32 devices in a mesh: rows: 16 (over z, y, x), seq: 2 (over core).
Axes of the slice: x: 2, y: 2, z: 4, core: 2. Of those that a mesh axis runs over, the one named last changes fastest.
Arguments:
- tokens: bfloat16 [16, 1024, 1024], P('rows', 'seq'), may hold values from -6 to 6
- noise_levels: float32 [16, 16], P('rows', 'seq'), may hold values from 0 to 1000
- frame_clip: int32 [16, 16], P('rows'), may hold values from 0 to 3, as said below
- w_qkv: bfloat16 [1024, 3, 1024], P('rows', None, 'seq'), may hold values from -0.1875 to 0.1875
- w_out: bfloat16 [1024, 1024], P('seq', 'rows'), may hold values from -1.5 to 1.5
- w_up: bfloat16 [1024, 4096], P('rows', 'seq'), may hold values from -0.1875 to 0.1875
- w_down: bfloat16 [4096, 1024], P('seq', 'rows'), may hold values from -0.09375 to 0.09375
- w_mod: bfloat16 [1024, 6144], P(None, 'seq'), may hold values from -0.1875 to 0.1875
- b_mod: bfloat16 [6144], P('seq'), may hold values from -4 to 4
- cotangent: bfloat16 [16, 1024, 1024], P('rows', 'seq'), may hold values from -6 to 6
Outputs:
- output: bfloat16 [16, 1024, 1024], P('rows', 'seq')
- grad_tokens: bfloat16 [16, 1024, 1024], P('rows', 'seq')
- grad_qkv: float32 [1024, 3, 1024], P('rows', None, 'seq')
- grad_out: float32 [1024, 1024], P('seq', 'rows')
- grad_up: float32 [1024, 4096], P('rows', 'seq')
- grad_down: float32 [4096, 1024], P('seq', 'rows')
- grad_mod: float32 [1024, 6144], P(None, 'seq')
- grad_bias: float32 [6144], P('seq')
The draws below stay inside these ranges and needn't reach their ends.
Inputs may be any that keep to these rules, and one draw needn't show every extreme that they name: `frame_clip`: in each row the clip numbers start at 0 and rise by one from clip to clip; a run of equal numbers is one clip of 4 to 16 frames, except that the frames after the row's last whole clip (padding, fewer than 16) carry the next number.
All inputs are finite; a program needn't handle non-finite values.
Results may differ from the reference program's by a relative error of at most 0.015.
Values may be sent and summed in bfloat16 or wider, within the bound.
No kernel may reach another device: no remote copies, remote signals or barrier semaphores. Data moves between devices by JAX's collectives and lax.ppermute only.
A program may use at most 320 MiB of HBM per device.

```python
import math
import jax
import jax.numpy as jnp
from jax import lax

D = 1024
HEADS = 16
HEAD = 64
FF = 4096
FRAME = 64
FRAMES_ROW = 16
ROW_LEN = 1024
ROWS = 16


def draw_frame_clip(key, part):
    longest = min(16, FRAMES_ROW)
    lengths = jax.random.randint(key, (ROWS, FRAMES_ROW), 4, longest + 1)
    first_row = (jnp.arange(ROWS) == 0)[:, None]
    lengths = jnp.where(first_row, 4, lengths).astype(jnp.int32)
    clip_ends = jnp.cumsum(lengths, axis=1)
    frames = jnp.arange(FRAMES_ROW)
    finished = (clip_ends[:, None, :] <= frames[None, :, None]) & (clip_ends[:, None, :] <= FRAMES_ROW)
    return jnp.sum(finished.astype(jnp.int32), axis=2).astype(jnp.int32)


def spiked(values, own_key, source, target, parts, factor):
    def block_of(position):
        return (jnp.arange(values.shape[position]) // (values.shape[position] // parts)).reshape((-1,) + (1,) * (values.ndim - 1 - position))

    one_side = jax.random.permutation(own_key, parts)[block_of(target)]
    second = (block_of(target) + parts // 2) % parts
    return jnp.where((block_of(source) == one_side) | (block_of(source) == second), factor * values, values)


def block_levels(key, extent, cuts, smallest, largest):
    level = 1.0
    for position, shards_of in cuts:
        heights = jax.random.uniform(jax.random.fold_in(jax.random.fold_in(key, 6), position), (shards_of,), jnp.float32, smallest / len(cuts), largest / len(cuts))
        level = level * jnp.repeat(jnp.exp(heights), extent[position] // shards_of).reshape((-1,) + (1,) * (len(extent) - 1 - position))
    return level


def centred(own_key, extent, deviation, limit, shards=(), held_as=jnp.bfloat16):
    array = jax.random.normal(own_key, extent, jnp.float32) * deviation
    if len(shards) > 0:
        array = block_levels(own_key, extent, shards, -0.22, 0.18) * array
    return jnp.clip(array, min=-limit, max=limit).astype(held_as)


def bell_draw_with(own_key, shape, deviation, bound, pieces, heavy, dtype=jnp.bfloat16):
    result = deviation * jax.random.normal(own_key, shape, jnp.float32)
    if pieces:
        result = result * block_levels(own_key, shape, pieces, -0.22, 0.18)
    return jnp.clip(spiked(result, jax.random.fold_in(own_key, 3), *heavy), -bound, bound).astype(dtype)


def setup_inputs(seed: int = 0) -> dict:
    seeds = jax.random.split(jax.random.key(seed), 11)
    return {
        "tokens": centred(seeds[0], (ROWS, ROW_LEN, D), 1.0, 6.0, ((0, 16), (1, 2))),
        "noise_levels": jnp.clip(1000.0 * jax.random.uniform(seeds[1], (ROWS, FRAMES_ROW), jnp.float32) ** block_levels(seeds[1], (ROWS, FRAMES_ROW), ((0, 16), (1, 2)), -0.2, 0.2), 0.0, 1000.0),
        "frame_clip": draw_frame_clip(jax.random.fold_in(seeds[10], 71), 0),
        "w_qkv": centred(seeds[3], (D, 3, D), D ** -0.5, 0.1875, ((0, 16), (2, 2))),
        "w_out": centred(seeds[4], (D, D), (D // 64) ** -0.5, 1.5, ((0, 2), (1, 16))),
        "w_up": centred(seeds[5], (D, FF), D ** -0.5, 0.1875, ((0, 16), (1, 2))),
        "w_down": centred(seeds[6], (FF, D), FF ** -0.5, 0.09375, ((0, 2), (1, 16))),
        "w_mod": centred(seeds[7], (D, 6 * D), D ** -0.5, 0.1875, ((1, 2),)),
        "b_mod": centred(seeds[8], (6 * D,), 1.0, 4.0, ((0, 2),)),
        "cotangent": bell_draw_with(seeds[9], (ROWS, ROW_LEN, D), 1.0, 6.0, ((0, 16), (1, 2)), (0, 2, 16, 2.0)),
    }


highest = lax.Precision.HIGHEST
norm_eps = 1e-06
masked_score = -1e+30

@jax.custom_vjp
def low(v):
    return lax.optimization_barrier(v.astype(jnp.bfloat16)).astype(jnp.float32)

@jax.custom_vjp
def low_back(v):
    return v

def low_keep(v):
    return (low(v), None)

def low_pass(kept, grad):
    return (grad,)

def back_keep(v):
    return (v, None)

def back_low(kept, grad):
    return (low(grad),)
low.defvjp(low_keep, low_pass)
low_back.defvjp(back_keep, back_low)

def noise_features(levels):
    half_width = D // 2
    frequency = jnp.exp(-math.log(10000.0) * jnp.arange(half_width).astype(jnp.float32) / half_width)
    angles = levels[..., None] * frequency
    return jax.nn.silu(jnp.concatenate([jnp.cos(angles), jnp.sin(angles)], axis=-1))

def normalize(values):
    centered = values - lax.optimization_barrier(jnp.mean(values, axis=-1, keepdims=True))
    return centered * lax.rsqrt(lax.optimization_barrier(jnp.mean(centered * centered, axis=-1, keepdims=True)) + norm_eps)

def row_forward(row_tokens, row_levels, row_clip, weights):
    w_qkv, w_out, w_up, w_down, w_mod, b_mod = weights
    length = row_tokens.shape[0]
    condition = low(noise_features(row_levels))
    modulation = jnp.repeat(jnp.dot(condition, w_mod, precision=highest) + b_mod, FRAME, axis=0)
    shift_attn, scale_attn, gate_attn, shift_mlp, scale_mlp, gate_mlp = jnp.split(modulation, 6, axis=-1)
    first_in = low(normalize(row_tokens) * (1.0 + scale_attn) + shift_attn)
    qkv_rows = low(low_back(jnp.dot(first_in, w_qkv.reshape(D, 3 * D), precision=highest)))
    queries, key_rows, values = [part_of.reshape(length, HEADS, HEAD) for part_of in jnp.split(qkv_rows, 3, axis=-1)]
    seg_tokens = jnp.repeat(row_clip, FRAME)
    frame_tokens = jnp.arange(length) // FRAME
    allowed = (seg_tokens[:, None] == seg_tokens[None, :]) & (frame_tokens[None, :] <= frame_tokens[:, None])
    scores = low_back(jnp.einsum('qhd,khd->hqk', queries, key_rows, precision=highest) * HEAD ** (-0.5))
    scores = jnp.where(allowed[None], scores, masked_score)
    probability = low(jax.nn.softmax(scores, axis=-1))
    attended = low(low_back(jnp.einsum('hqk,khd->qhd', probability, values, precision=highest).reshape(length, D)))
    branch = low_back(jnp.dot(attended, w_out, precision=highest))
    middle = row_tokens + gate_attn * branch
    second_in = low(normalize(middle) * (1.0 + scale_mlp) + shift_mlp)
    hidden_pre = low_back(jnp.dot(second_in, w_up, precision=highest))
    hidden = low(jax.nn.gelu(hidden_pre, approximate=True))
    mlp_out = low_back(jnp.dot(hidden, w_down, precision=highest))
    return middle + gate_mlp * mlp_out

def reference(tokens, noise_levels, frame_clip, w_qkv, w_out, w_up, w_down, w_mod, b_mod, cotangent):
    weights = (w_qkv.astype(jnp.float32), w_out.astype(jnp.float32), w_up.astype(jnp.float32), w_down.astype(jnp.float32), w_mod.astype(jnp.float32), b_mod.astype(jnp.float32))
    levels = noise_levels.astype(jnp.float32)

    def forward(all_tokens, all_weights):

        def one_row(row_tokens, row_levels, row_clip):
            return row_forward(row_tokens, row_levels, row_clip, all_weights)
        checked = jax.checkpoint(one_row)

        def scan_step(running, packed):
            return (running, checked(packed[0], packed[1], packed[2]))
        unused, rows_out = lax.scan(scan_step, jnp.zeros((), jnp.float32), (all_tokens, levels, frame_clip))
        return rows_out
    output, pullback = jax.vjp(forward, tokens.astype(jnp.float32), weights)
    grad_tokens, grad_weights = pullback(cotangent.astype(jnp.float32))
    return (output.astype(jnp.bfloat16), grad_tokens.astype(jnp.bfloat16), grad_weights[0], grad_weights[1], grad_weights[2], grad_weights[3], grad_weights[4], grad_weights[5])
```

```python
import math

import jax
import jax.numpy as jnp
from jax import lax
from jax.experimental import pallas as pl
from jax.experimental.pallas import tpu as pltpu
from jax.sharding import PartitionSpec as P

D = 1024
HEAD = 64
FRAME = 64
PAIR = 2 * HEAD
QB = 256

norm_eps = 1e-06
hidden_score = -1e30


f32 = jnp.float32
bf16 = jnp.bfloat16


def noise_features(levels):
    half_width = D // 2
    frequency = jnp.exp(
        -math.log(10000.0) * jnp.arange(half_width).astype(jnp.float32) / half_width
    )
    angles = levels[..., None] * frequency
    return jax.nn.silu(jnp.concatenate([jnp.cos(angles), jnp.sin(angles)], axis=-1))


def normalize(values):
    centered = values - jnp.mean(values, axis=-1, keepdims=True)
    return centered * lax.rsqrt(jnp.mean(centered * centered, axis=-1, keepdims=True) + norm_eps)


def modulated(values, offsets, factors):
    return normalize(values) * (1.0 + factors) + offsets


def gelu_tanh(values):
    return jax.nn.gelu(values, approximate=True)


def grid_of(count):
    deep = 4
    side = math.isqrt(count // deep)
    return (deep, side, side)


def shift_pairs(grid, axis, amount):
    pairs = []
    for z in range(grid[0]):
        for y in range(grid[1]):
            for x in range(grid[2]):
                to = [z, y, x]
                to[axis] = (to[axis] + amount) % grid[axis]
                pairs.append(
                    (
                        (z * grid[1] + y) * grid[2] + x,
                        (to[0] * grid[1] + to[1]) * grid[2] + to[2],
                    )
                )
    return pairs


def place_on(grid):
    me = lax.axis_index("rows")
    return (me // (grid[1] * grid[2]), (me // grid[2]) % grid[1], me % grid[2])


def gather_axis(part, grid, axis, at, dim):
    count = grid[axis]
    whole = jnp.zeros(part.shape[:dim] + (count,) + part.shape[dim:], part.dtype)
    pieces = [part] + [
        lax.ppermute(part, "rows", shift_pairs(grid, axis, k)) for k in range(1, count)
    ]
    for k, piece in enumerate(pieces):
        whole = lax.dynamic_update_index_in_dim(whole, piece, (at[axis] - k) % count, dim)
    return whole


def gather_deep(shard, grid, at):
    return gather_axis(shard, grid, 0, at, 0)


def gather_rest(deep, grid, at):
    cut = deep.shape[-1] // 2
    first = gather_axis(deep[..., :cut], grid, 2, at, 1)
    first = gather_axis(first, grid, 1, at, 1)
    second = gather_axis(deep[..., cut:], grid, 1, at, 1)
    second = gather_axis(second, grid, 2, at, 2)
    whole = jnp.concatenate([first, second], axis=-1)
    return whole.reshape(-1, whole.shape[-1])


def scatter_axis(whole, grid, axis, at, dim):
    count = grid[axis]
    total = lax.dynamic_index_in_dim(whole, at[axis], dim, keepdims=False).astype(f32)
    for k in range(1, count):
        piece = lax.dynamic_index_in_dim(whole, (at[axis] + k) % count, dim, keepdims=False)
        total = total + lax.ppermute(piece, "rows", shift_pairs(grid, axis, k)).astype(f32)
    return total


def scatter_rows(whole, grid, at):
    cols = whole.shape[-1]
    cut = cols // 2
    view = whole.reshape(*grid, -1, cols)
    first = scatter_axis(view[..., :cut], grid, 1, at, 1).astype(bf16)
    first = scatter_axis(first, grid, 2, at, 1).astype(bf16)
    second = scatter_axis(view[..., cut:], grid, 2, at, 2).astype(bf16)
    second = scatter_axis(second, grid, 1, at, 1).astype(bf16)
    return jnp.concatenate(
        [scatter_axis(first, grid, 0, at, 0), scatter_axis(second, grid, 0, at, 0)], axis=-1
    )


def swapped(part):
    return lax.ppermute(part, "seq", [(0, 1), (1, 0)])


def in_order(own, other, side):
    whole = jnp.zeros((2 * own.shape[0],) + own.shape[1:], own.dtype)
    half = own.shape[0]
    whole = lax.dynamic_update_slice_in_dim(whole, own, side * half, 0)
    return lax.dynamic_update_slice_in_dim(whole, other, (1 - side) * half, 0)


def half_of(whole, which):
    half = whole.shape[0] // 2
    return lax.dynamic_slice_in_dim(whole, which * half, half, 0)


def nt(a, b):
    return lax.dot_general(a, b, (((1,), (1,)), ((), ())), preferred_element_type=f32)


def nn(a, b):
    return lax.dot_general(a, b, (((1,), (0,)), ((), ())), preferred_element_type=f32)


def lane_in(shape, head):
    lanes = lax.broadcasted_iota(jnp.int32, shape, 1)
    return (lanes // HEAD) == head


def forward_kernel(qkv_ref, seen_ref, frame_ref, out_ref, log_ref):
    length = qkv_ref.shape[0]
    queries = qkv_ref[:, 0:PAIR] * jnp.asarray(HEAD**-0.5, bf16)
    keys = qkv_ref[:, PAIR : 2 * PAIR]
    values_t = qkv_ref[:, 2 * PAIR : 3 * PAIR].T
    seen = seen_ref[...]
    frames = frame_ref[...]
    own = [lane_in((length, PAIR), head) for head in range(2)]
    query_h = [jnp.where(own[head], queries, seen) for head in range(2)]
    key_h = [jnp.where(own[head], keys, frames) for head in range(2)]
    for start in range(0, length, QB):
        stop = start + QB
        parts = []
        for head in range(2):
            scores = nt(key_h[head][:stop], query_h[head][start:stop])
            largest = jnp.max(scores, axis=0, keepdims=True)
            exponent = jnp.exp(scores - largest)
            denominator = jnp.sum(exponent, axis=0, keepdims=True)
            combined = nn(values_t[head * HEAD : (head + 1) * HEAD, :stop], exponent.astype(bf16))
            parts.append(combined / denominator)
            log_ref[0, head : head + 1, start:stop] = largest + jnp.log(denominator)
        out_ref[start:stop, :] = jnp.concatenate(parts, axis=0).T.astype(bf16)


def backward_kernel(qkv_ref, seen_ref, frame_ref, log_ref, grad_ref, out_ref, key_sum, value_sum):
    length = qkv_ref.shape[0]
    queries = qkv_ref[:, 0:PAIR] * jnp.asarray(HEAD**-0.5, bf16)
    keys = qkv_ref[:, PAIR : 2 * PAIR]
    values = qkv_ref[:, 2 * PAIR : 3 * PAIR]
    grads = grad_ref[...]
    keys_t = keys.T
    seen = seen_ref[...]
    frames = frame_ref[...]
    nothing = jnp.zeros((length, PAIR), bf16)
    own = [lane_in((length, PAIR), head) for head in range(2)]
    query_h = [jnp.where(own[head], queries, seen) for head in range(2)]
    query_only = [jnp.where(own[head], queries, nothing) for head in range(2)]
    key_h = [jnp.where(own[head], keys, frames) for head in range(2)]
    grad_h = [jnp.where(own[head], grads, nothing) for head in range(2)]
    for start in reversed(range(0, length, QB)):
        stop = start + QB
        query_parts = []
        for head in range(2):
            grad_block = grad_h[head][start:stop]
            scores = nt(key_h[head][:stop], query_h[head][start:stop])
            chance = jnp.exp(scores - log_ref[0, head : head + 1, start:stop])
            grad_chance = nt(values[:stop], grad_block)
            product = chance * grad_chance
            grad_scores = product - chance * jnp.sum(product, axis=0, keepdims=True)
            grad_scores = grad_scores.astype(bf16)
            value_part = nn(chance.astype(bf16), grad_block)
            key_part = nn(grad_scores, query_only[head][start:stop])
            if stop == length and head == 0:
                value_sum[...] = value_part
                key_sum[...] = key_part
            else:
                value_sum[:stop, :] += value_part
                key_sum[:stop, :] += key_part
            query_parts.append(nn(keys_t[head * HEAD : (head + 1) * HEAD, :stop], grad_scores))
        query_grad = jnp.concatenate(query_parts, axis=0).T * HEAD**-0.5
        out_ref[start:stop, 0:PAIR] = query_grad.astype(bf16)
    out_ref[:, PAIR : 2 * PAIR] = key_sum[...].astype(bf16)
    out_ref[:, 2 * PAIR : 3 * PAIR] = value_sum[...].astype(bf16)


def attend(qkv, seen, frames):
    length, cols = qkv.shape
    pairs = cols // (3 * PAIR)
    whole = pl.BlockSpec((length, PAIR), lambda p: (0, 0))
    return pl.pallas_call(
        forward_kernel,
        grid=(pairs,),
        in_specs=[pl.BlockSpec((length, 3 * PAIR), lambda p: (0, p)), whole, whole],
        out_specs=[
            pl.BlockSpec((length, PAIR), lambda p: (0, p)),
            pl.BlockSpec((1, 2, length), lambda p: (p, 0, 0)),
        ],
        out_shape=[
            jax.ShapeDtypeStruct((length, pairs * PAIR), bf16),
            jax.ShapeDtypeStruct((pairs, 2, length), f32),
        ],
        cost_estimate=pl.CostEstimate(
            flops=8 * pairs * length * length * HEAD,
            bytes_accessed=8 * pairs * length * PAIR,
            transcendentals=2 * pairs * length * length,
        ),
        name="attend",
    )(qkv, seen, frames)


def attend_back(qkv, seen, frames, logs, grads, first, pairs):
    length = qkv.shape[0]
    whole = pl.BlockSpec((length, PAIR), lambda p: (0, 0))
    return pl.pallas_call(
        backward_kernel,
        grid=(pairs,),
        in_specs=[
            pl.BlockSpec((length, 3 * PAIR), lambda p: (0, p + first)),
            whole,
            whole,
            pl.BlockSpec((1, 2, length), lambda p: (p + first, 0, 0)),
            pl.BlockSpec((length, PAIR), lambda p: (0, p + first)),
        ],
        out_specs=pl.BlockSpec((length, 3 * PAIR), lambda p: (0, p)),
        out_shape=jax.ShapeDtypeStruct((length, pairs * 3 * PAIR), bf16),
        scratch_shapes=[pltpu.VMEM((length, PAIR), f32), pltpu.VMEM((length, PAIR), f32)],
        cost_estimate=pl.CostEstimate(
            flops=20 * pairs * length * length * HEAD,
            bytes_accessed=14 * pairs * length * PAIR,
            transcendentals=2 * pairs * length * length,
        ),
        name="attend_back",
    )(qkv, seen, frames, logs, grads)


def frame_lanes(per_frame):
    frames = per_frame.shape[0]
    padded = jnp.pad(per_frame.astype(bf16), ((0, 0), (0, HEAD - frames)))
    return jnp.repeat(jnp.concatenate([padded, padded], axis=1), FRAME, axis=0)


def shards(tokens, noise_levels, frame_clip, w_qkv, w_out, w_up, w_down, w_mod, b_mod, cotangent):
    rows_here, local_len, width = tokens.shape
    frames_here = noise_levels.shape[1]
    grid = grid_of(lax.axis_size("rows"))
    at = place_on(grid)
    side = lax.axis_index("seq")
    share = w_qkv.shape[0]
    head_cols = w_qkv.shape[2]
    pairs = head_cols // PAIR
    hidden_cols = w_up.shape[1]

    qkv_share = (
        w_qkv.reshape(share, 3, pairs, PAIR).transpose(0, 2, 1, 3).reshape(share, 3 * head_cols)
    )
    rest_share = jnp.concatenate([w_out.T, w_up], axis=1)
    down_share = w_down.T
    qkv_deep = gather_deep(qkv_share, grid, at)
    rest_share, down_share, qkv_deep = lax.optimization_barrier(
        (rest_share, down_share, qkv_deep)
    )
    qkv_whole = gather_rest(qkv_deep, grid, at)
    rest_deep = gather_deep(rest_share, grid, at)
    down_share, rest_deep = lax.optimization_barrier((down_share, rest_deep))
    rest_whole = gather_rest(rest_deep, grid, at)
    out_whole = rest_whole[:, :head_cols]
    up_whole = rest_whole[:, head_cols:]
    down_whole = gather_rest(gather_deep(down_share, grid, at), grid, at)

    levels = in_order(noise_levels[0], swapped(noise_levels[0]), side)
    condition = noise_features(levels).astype(bf16)
    mod_cols = jnp.dot(condition, w_mod, preferred_element_type=f32) + b_mod.astype(f32)
    own_cols = half_of(mod_cols, side)
    other_cols = swapped(half_of(mod_cols, 1 - side))
    modulation = in_order(
        own_cols.reshape(frames_here, 3, width).transpose(1, 0, 2),
        other_cols.reshape(frames_here, 3, width).transpose(1, 0, 2),
        side,
    )[:, :, None]
    shift_attn, scale_attn, gate_attn, shift_mlp, scale_mlp, gate_mlp = [
        modulation[k] for k in range(6)
    ]
    condition_all = lax.all_gather(condition, "rows", axis=0, tiled=True)

    framed = tokens[0].astype(f32).reshape(frames_here, FRAME, width)
    upstream = cotangent[0].astype(f32).reshape(frames_here, FRAME, width)
    first_own = modulated(framed, shift_attn, scale_attn).astype(bf16).reshape(local_len, width)
    first_full = in_order(first_own, swapped(first_own), side)
    grad_mlp = (gate_mlp * upstream).astype(bf16).reshape(local_len, width)
    grad_mlp_full = jnp.concatenate([grad_mlp, swapped(grad_mlp)], axis=0)

    clip = frame_clip[0]
    order = jnp.arange(clip.shape[0])
    visible = (clip[:, None] == clip[None, :]) & (order[None, :] <= order[:, None])
    seen = frame_lanes(jnp.where(visible, 0.0, hidden_score))
    frames = frame_lanes(jnp.eye(clip.shape[0]))

    qkv = jnp.dot(first_full, qkv_whole, preferred_element_type=f32).astype(bf16)
    attended, logs = attend(qkv, seen, frames)
    branch_other = swapped(nt(half_of(attended, 1 - side), out_whole).astype(bf16))
    branch = nt(half_of(attended, side), out_whole) + branch_other.astype(f32)
    branch = branch.reshape(framed.shape)
    middle = framed + gate_attn * branch
    second_own = modulated(middle, shift_mlp, scale_mlp).astype(bf16).reshape(local_len, width)
    second_full = jnp.concatenate([second_own, swapped(second_own)], axis=0)
    hidden_pre = jnp.dot(second_full, up_whole, preferred_element_type=f32)
    hidden = gelu_tanh(hidden_pre).astype(bf16)
    mlp_other = swapped(nt(hidden[local_len:], down_whole).astype(bf16))
    mlp_out = (nt(hidden[:local_len], down_whole) + mlp_other.astype(f32)).reshape(framed.shape)
    output = (middle + gate_mlp * mlp_out).astype(bf16).reshape(tokens.shape)
    grad_gate_mlp = jnp.sum(upstream * mlp_out, axis=1)

    def tn(a, b):
        return lax.dot_general(a, b, (((0,), (0,)), ((), ())), preferred_element_type=f32)

    down_sum = scatter_rows(tn(grad_mlp_full, hidden).astype(bf16), grid, at)
    grad_hidden = jnp.dot(grad_mlp_full, down_whole, preferred_element_type=f32)
    grad_pre = jax.vjp(gelu_tanh, hidden_pre)[1](grad_hidden)[0].astype(bf16)
    second_other = swapped(nt(grad_pre[local_len:], up_whole).astype(bf16))
    grad_second = nt(grad_pre[:local_len], up_whole) + second_other.astype(f32)
    up_sum = scatter_rows(tn(second_full, grad_pre).astype(bf16), grid, at)
    second_back = jax.vjp(modulated, middle, shift_mlp, scale_mlp)[1]
    grad_middle, grad_shift_mlp, grad_scale_mlp = second_back(grad_second.reshape(framed.shape))
    grad_middle = grad_middle + upstream
    grad_gate_attn = jnp.sum(grad_middle * branch, axis=1)
    grad_branch = (gate_attn * grad_middle).astype(bf16).reshape(local_len, width)
    branch_full = in_order(grad_branch, swapped(grad_branch), side)
    out_sum = scatter_rows(tn(branch_full, attended).astype(bf16), grid, at)
    grad_attended = jnp.dot(branch_full, out_whole, preferred_element_type=f32).astype(bf16)
    halves = 2 if pairs % 2 == 0 else 1
    count = pairs // halves
    grad_qkv, qkv_sums = [], []
    for k in range(halves):
        part = attend_back(qkv, seen, frames, logs, grad_attended, k * count, count)
        grad_qkv.append(part)
        qkv_sums.append(scatter_rows(tn(first_full, part).astype(bf16), grid, at))
    wide = count * 3 * PAIR

    def first_part(which):
        return sum(
            nt(half_of(grad_qkv[k], which), qkv_whole[:, k * wide : (k + 1) * wide])
            for k in range(halves)
        )

    first_other = swapped(first_part(1 - side).astype(bf16))
    grad_first = first_part(side) + first_other.astype(f32)
    first_back = jax.vjp(modulated, framed, shift_attn, scale_attn)[1]
    grad_framed, grad_shift_attn, grad_scale_attn = first_back(grad_first.reshape(framed.shape))
    grad_tokens = (grad_framed + grad_middle).astype(bf16).reshape(tokens.shape)

    def columns(low, high):
        low, high = low.reshape(frames_here, -1), high.reshape(frames_here, -1)
        keep = jnp.where(side == 0, low, high).astype(bf16)
        give = jnp.where(side == 0, high, low).astype(bf16)
        mine = in_order(keep, swapped(give), side)
        return lax.all_gather(mine, "rows", axis=0, tiled=True)

    gates = columns(grad_gate_attn, grad_gate_mlp)
    pairs_late = columns(
        jnp.concatenate([grad_shift_attn, grad_scale_attn], axis=-1),
        jnp.concatenate([grad_shift_mlp, grad_scale_mlp], axis=-1),
    )
    grad_mods = jnp.concatenate([pairs_late, gates], axis=1)
    mod_sum = tn(condition_all, grad_mods)
    bias_sum = jnp.sum(grad_mods.astype(f32), axis=0)

    qkv_sum = jnp.concatenate(qkv_sums, axis=1)
    qkv_sum = qkv_sum.reshape(share, pairs, 3, PAIR).transpose(0, 2, 1, 3).reshape(w_qkv.shape)
    return (output, grad_tokens, qkv_sum, out_sum.T, up_sum, down_sum.T, mod_sum, bias_sum)


def solution(mesh):
    in_specs = (
        P("rows", "seq", None),
        P("rows", "seq"),
        P("rows", None),
        P("rows", None, "seq"),
        P("seq", "rows"),
        P("rows", "seq"),
        P("seq", "rows"),
        P(None, "seq"),
        P("seq"),
        P("rows", "seq", None),
    )
    out_specs = (
        P("rows", "seq", None),
        P("rows", "seq", None),
        P("rows", None, "seq"),
        P("seq", "rows"),
        P("rows", "seq"),
        P("seq", "rows"),
        P(None, "seq"),
        P("seq"),
    )
    return jax.shard_map(shards, mesh=mesh, in_specs=in_specs, out_specs=out_specs, check_vma=False)
```

```python
import math

import jax
import jax.numpy as jnp
from jax import lax
from jax.experimental import pallas as pl
from jax.experimental.pallas import tpu as pltpu
from jax.sharding import PartitionSpec as P

D = 1024
HEAD = 64
FRAME = 64
PAIR = 2 * HEAD
QB = 256

norm_eps = 1e-06
hidden_score = -1e30


f32 = jnp.float32
bf16 = jnp.bfloat16


def noise_features(levels):
    half_width = D // 2
    frequency = jnp.exp(
        -math.log(10000.0) * jnp.arange(half_width).astype(jnp.float32) / half_width
    )
    angles = levels[..., None] * frequency
    return jax.nn.silu(jnp.concatenate([jnp.cos(angles), jnp.sin(angles)], axis=-1))


def normalize(values):
    centered = values - jnp.mean(values, axis=-1, keepdims=True)
    return centered * lax.rsqrt(jnp.mean(centered * centered, axis=-1, keepdims=True) + norm_eps)


def modulated(values, offsets, factors):
    return normalize(values) * (1.0 + factors) + offsets


def gelu_tanh(values):
    return jax.nn.gelu(values, approximate=True)


def grid_of(count):
    deep = 4
    side = math.isqrt(count // deep)
    return (deep, side, side)


def shift_pairs(grid, axis, amount):
    pairs = []
    for z in range(grid[0]):
        for y in range(grid[1]):
            for x in range(grid[2]):
                to = [z, y, x]
                to[axis] = (to[axis] + amount) % grid[axis]
                pairs.append(
                    (
                        (z * grid[1] + y) * grid[2] + x,
                        (to[0] * grid[1] + to[1]) * grid[2] + to[2],
                    )
                )
    return pairs


def place_on(grid):
    me = lax.axis_index("rows")
    return (me // (grid[1] * grid[2]), (me // grid[2]) % grid[1], me % grid[2])


def gather_axis(part, grid, axis, at, dim):
    count = grid[axis]
    whole = jnp.zeros(part.shape[:dim] + (count,) + part.shape[dim:], part.dtype)
    pieces = [part] + [
        lax.ppermute(part, "rows", shift_pairs(grid, axis, k)) for k in range(1, count)
    ]
    for k, piece in enumerate(pieces):
        whole = lax.dynamic_update_index_in_dim(whole, piece, (at[axis] - k) % count, dim)
    return whole


def gather_deep(shard, grid, at):
    return gather_axis(shard, grid, 0, at, 0)


def gather_rest(deep, grid, at):
    cut = deep.shape[-1] // 2
    first = gather_axis(deep[..., :cut], grid, 2, at, 1)
    first = gather_axis(first, grid, 1, at, 1)
    second = gather_axis(deep[..., cut:], grid, 1, at, 1)
    second = gather_axis(second, grid, 2, at, 2)
    whole = jnp.concatenate([first, second], axis=-1)
    return whole.reshape(-1, whole.shape[-1])


def pieces_of(whole, grid, axis, at, dim):
    return [
        lax.dynamic_index_in_dim(whole, (at[axis] + k) % grid[axis], dim, keepdims=False)
        for k in range(grid[axis])
    ]


def sum_pieces(pieces, grid, axis):
    total = pieces[0].astype(f32)
    for k in range(1, grid[axis]):
        total = total + lax.ppermute(pieces[k], "rows", shift_pairs(grid, axis, k)).astype(f32)
    return total


def scatter_axis(whole, grid, axis, at, dim):
    return sum_pieces(pieces_of(whole, grid, axis, at, dim), grid, axis)


def scatter_cut(whole, grid, at):
    cols = whole.shape[-1]
    cut = cols // 2
    view = whole.reshape(*grid, -1, cols)
    return (
        pieces_of(view[..., :cut], grid, 1, at, 1),
        pieces_of(view[..., cut:], grid, 2, at, 2),
    )


def scatter_rows(cuts, grid, at):
    first = sum_pieces(cuts[0], grid, 1).astype(bf16)
    second = sum_pieces(cuts[1], grid, 2).astype(bf16)
    first = scatter_axis(first, grid, 2, at, 1).astype(bf16)
    second = scatter_axis(second, grid, 1, at, 1).astype(bf16)
    return scatter_axis(jnp.concatenate([first, second], axis=-1), grid, 0, at, 0)


def swapped(part):
    return lax.ppermute(part, "seq", [(0, 1), (1, 0)])


def in_order(own, other, side):
    whole = jnp.zeros((2 * own.shape[0],) + own.shape[1:], own.dtype)
    half = own.shape[0]
    whole = lax.dynamic_update_slice_in_dim(whole, own, side * half, 0)
    return lax.dynamic_update_slice_in_dim(whole, other, (1 - side) * half, 0)


def half_of(whole, which):
    half = whole.shape[0] // 2
    return lax.dynamic_slice_in_dim(whole, which * half, half, 0)


def nt(a, b):
    return lax.dot_general(a, b, (((1,), (1,)), ((), ())), preferred_element_type=f32)


def nn(a, b):
    return lax.dot_general(a, b, (((1,), (0,)), ((), ())), preferred_element_type=f32)


def lane_in(shape, head):
    lanes = lax.broadcasted_iota(jnp.int32, shape, 1)
    return (lanes // HEAD) == head


def forward_kernel(qkv_ref, seen_ref, frame_ref, out_ref, log_ref):
    length = qkv_ref.shape[0]
    queries = qkv_ref[:, 0:PAIR] * jnp.asarray(HEAD**-0.5, bf16)
    keys = qkv_ref[:, PAIR : 2 * PAIR]
    values_t = qkv_ref[:, 2 * PAIR : 3 * PAIR].T
    seen = seen_ref[...]
    frames = frame_ref[...]
    own = [lane_in((length, PAIR), head) for head in range(2)]
    query_h = [jnp.where(own[head], queries, seen) for head in range(2)]
    key_h = [jnp.where(own[head], keys, frames) for head in range(2)]
    for start in range(0, length, QB):
        stop = start + QB
        parts = []
        for head in range(2):
            scores = nt(key_h[head][:stop], query_h[head][start:stop])
            largest = jnp.max(scores, axis=0, keepdims=True)
            exponent = jnp.exp(scores - largest)
            denominator = jnp.sum(exponent, axis=0, keepdims=True)
            combined = nn(values_t[head * HEAD : (head + 1) * HEAD, :stop], exponent.astype(bf16))
            parts.append(combined / denominator)
            log_ref[0, head : head + 1, start:stop] = largest + jnp.log(denominator)
        out_ref[start:stop, :] = jnp.concatenate(parts, axis=0).T.astype(bf16)


def backward_kernel(qkv_ref, seen_ref, frame_ref, log_ref, grad_ref, out_ref, key_sum, value_sum):
    length = qkv_ref.shape[0]
    queries = qkv_ref[:, 0:PAIR] * jnp.asarray(HEAD**-0.5, bf16)
    keys = qkv_ref[:, PAIR : 2 * PAIR]
    values = qkv_ref[:, 2 * PAIR : 3 * PAIR]
    grads = grad_ref[...]
    keys_t = keys.T
    seen = seen_ref[...]
    frames = frame_ref[...]
    nothing = jnp.zeros((length, PAIR), bf16)
    own = [lane_in((length, PAIR), head) for head in range(2)]
    query_h = [jnp.where(own[head], queries, seen) for head in range(2)]
    query_only = [jnp.where(own[head], queries, nothing) for head in range(2)]
    key_h = [jnp.where(own[head], keys, frames) for head in range(2)]
    grad_h = [jnp.where(own[head], grads, nothing) for head in range(2)]
    for start in reversed(range(0, length, QB)):
        stop = start + QB
        query_parts = []
        for head in range(2):
            grad_block = grad_h[head][start:stop]
            scores = nt(key_h[head][:stop], query_h[head][start:stop])
            chance = jnp.exp(scores - log_ref[0, head : head + 1, start:stop])
            grad_chance = nt(values[:stop], grad_block)
            product = chance * grad_chance
            grad_scores = product - chance * jnp.sum(product, axis=0, keepdims=True)
            grad_scores = grad_scores.astype(bf16)
            value_part = nn(chance.astype(bf16), grad_block)
            key_part = nn(grad_scores, query_only[head][start:stop])
            if stop == length and head == 0:
                value_sum[...] = value_part
                key_sum[...] = key_part
            else:
                value_sum[:stop, :] += value_part
                key_sum[:stop, :] += key_part
            query_parts.append(nn(keys_t[head * HEAD : (head + 1) * HEAD, :stop], grad_scores))
        query_grad = jnp.concatenate(query_parts, axis=0).T * HEAD**-0.5
        out_ref[start:stop, 0:PAIR] = query_grad.astype(bf16)
    out_ref[:, PAIR : 2 * PAIR] = key_sum[...].astype(bf16)
    out_ref[:, 2 * PAIR : 3 * PAIR] = value_sum[...].astype(bf16)


def attend(qkv, seen, frames):
    length, cols = qkv.shape
    pairs = cols // (3 * PAIR)
    whole = pl.BlockSpec((length, PAIR), lambda p: (0, 0))
    return pl.pallas_call(
        forward_kernel,
        grid=(pairs,),
        in_specs=[pl.BlockSpec((length, 3 * PAIR), lambda p: (0, p)), whole, whole],
        out_specs=[
            pl.BlockSpec((length, PAIR), lambda p: (0, p)),
            pl.BlockSpec((1, 2, length), lambda p: (p, 0, 0)),
        ],
        out_shape=[
            jax.ShapeDtypeStruct((length, pairs * PAIR), bf16),
            jax.ShapeDtypeStruct((pairs, 2, length), f32),
        ],
        cost_estimate=pl.CostEstimate(
            flops=8 * pairs * length * length * HEAD,
            bytes_accessed=8 * pairs * length * PAIR,
            transcendentals=2 * pairs * length * length,
        ),
        name="attend",
    )(qkv, seen, frames)


def attend_back(qkv, seen, frames, logs, grads):
    length, cols = qkv.shape
    pairs = cols // (3 * PAIR)
    whole = pl.BlockSpec((length, PAIR), lambda p: (0, 0))
    return pl.pallas_call(
        backward_kernel,
        grid=(pairs,),
        in_specs=[
            pl.BlockSpec((length, 3 * PAIR), lambda p: (0, p)),
            whole,
            whole,
            pl.BlockSpec((1, 2, length), lambda p: (p, 0, 0)),
            pl.BlockSpec((length, PAIR), lambda p: (0, p)),
        ],
        out_specs=pl.BlockSpec((length, 3 * PAIR), lambda p: (0, p)),
        out_shape=jax.ShapeDtypeStruct((length, pairs * 3 * PAIR), bf16),
        scratch_shapes=[pltpu.VMEM((length, PAIR), f32), pltpu.VMEM((length, PAIR), f32)],
        cost_estimate=pl.CostEstimate(
            flops=20 * pairs * length * length * HEAD,
            bytes_accessed=14 * pairs * length * PAIR,
            transcendentals=2 * pairs * length * length,
        ),
        name="attend_back",
    )(qkv, seen, frames, logs, grads)


def frame_lanes(per_frame):
    frames = per_frame.shape[0]
    padded = jnp.pad(per_frame.astype(bf16), ((0, 0), (0, HEAD - frames)))
    return jnp.repeat(jnp.concatenate([padded, padded], axis=1), FRAME, axis=0)


def block(tokens, noise_levels, frame_clip, w_qkv, w_out, w_up, w_down, w_mod, b_mod, cotangent):
    _, local_len, width = tokens.shape
    frames_here = noise_levels.shape[1]
    grid = grid_of(lax.axis_size("rows"))
    at = place_on(grid)
    side = lax.axis_index("seq")
    share = w_qkv.shape[0]
    head_cols = w_qkv.shape[2]
    pairs = head_cols // PAIR

    qkv_share = (
        w_qkv.reshape(share, 3, pairs, PAIR).transpose(0, 2, 1, 3).reshape(share, 3 * head_cols)
    )
    levels = in_order(noise_levels[0], swapped(noise_levels[0]), side)
    condition = noise_features(levels).astype(bf16)
    condition_cols = condition.size // share
    rest_share = jnp.concatenate(
        [w_out.T, condition.reshape(share, condition_cols), w_up], axis=1
    )
    down_share = w_down.T
    qkv_deep = gather_deep(qkv_share, grid, at)
    rest_share, down_share, qkv_deep = lax.optimization_barrier(
        (rest_share, down_share, qkv_deep)
    )
    qkv_whole = gather_rest(qkv_deep, grid, at)
    down_whole = lax.all_gather(down_share, "rows", axis=0, tiled=True)
    rest_whole = gather_rest(gather_deep(rest_share, grid, at), grid, at)
    out_whole = rest_whole[:, :head_cols]
    up_whole = rest_whole[:, head_cols + condition_cols :]
    condition_all = rest_whole[:, head_cols : head_cols + condition_cols].reshape(-1, width)

    mod_cols = jnp.dot(condition, w_mod, preferred_element_type=f32) + b_mod.astype(f32)
    own_cols = half_of(mod_cols, side)
    other_cols = swapped(half_of(mod_cols, 1 - side))
    modulation = in_order(
        own_cols.reshape(frames_here, 3, width).transpose(1, 0, 2),
        other_cols.reshape(frames_here, 3, width).transpose(1, 0, 2),
        side,
    )[:, :, None]
    shift_attn, scale_attn, gate_attn, shift_mlp, scale_mlp, gate_mlp = [
        modulation[k] for k in range(6)
    ]

    framed = tokens[0].astype(f32).reshape(frames_here, FRAME, width)
    upstream = cotangent[0].astype(f32).reshape(frames_here, FRAME, width)
    first_own = modulated(framed, shift_attn, scale_attn).astype(bf16).reshape(local_len, width)
    first_full = in_order(first_own, swapped(first_own), side)
    grad_mlp = (gate_mlp * upstream).astype(bf16).reshape(local_len, width)
    grad_mlp_full = jnp.concatenate([grad_mlp, swapped(grad_mlp)], axis=0)

    clip = frame_clip[0]
    order = jnp.arange(clip.shape[0])
    visible = (clip[:, None] == clip[None, :]) & (order[None, :] <= order[:, None])
    seen = frame_lanes(jnp.where(visible, 0.0, hidden_score))
    frames = frame_lanes(jnp.eye(clip.shape[0]))

    qkv = jnp.dot(first_full, qkv_whole, preferred_element_type=f32).astype(bf16)
    attended, logs = attend(qkv, seen, frames)
    branch_other = swapped(nt(half_of(attended, 1 - side), out_whole).astype(bf16))
    branch = nt(half_of(attended, side), out_whole) + branch_other.astype(f32)
    branch = branch.reshape(framed.shape)
    middle = framed + gate_attn * branch
    second_own = modulated(middle, shift_mlp, scale_mlp).astype(bf16).reshape(local_len, width)
    second_full = jnp.concatenate([second_own, swapped(second_own)], axis=0)
    hidden_pre = jnp.dot(second_full, up_whole, preferred_element_type=f32)
    hidden = gelu_tanh(hidden_pre).astype(bf16)
    mlp_other = swapped(nt(hidden[local_len:], down_whole).astype(bf16))
    mlp_out = (nt(hidden[:local_len], down_whole) + mlp_other.astype(f32)).reshape(framed.shape)
    output = (middle + gate_mlp * mlp_out).astype(bf16).reshape(tokens.shape)
    grad_gate_mlp = jnp.sum(upstream * mlp_out, axis=1)

    def tn(a, b):
        return lax.dot_general(a, b, (((0,), (0,)), ((), ())), preferred_element_type=f32)

    down_sum = lax.psum_scatter(
        tn(grad_mlp_full, hidden).astype(bf16), "rows", scatter_dimension=0, tiled=True
    ).astype(f32)
    grad_hidden = jnp.dot(grad_mlp_full, down_whole, preferred_element_type=f32)
    grad_pre = jax.vjp(gelu_tanh, hidden_pre)[1](grad_hidden)[0].astype(bf16)
    second_other = swapped(nt(grad_pre[local_len:], up_whole).astype(bf16))
    grad_second = nt(grad_pre[:local_len], up_whole) + second_other.astype(f32)
    up_cuts = scatter_cut(tn(second_full, grad_pre).astype(bf16), grid, at)
    second_back = jax.vjp(modulated, middle, shift_mlp, scale_mlp)[1]
    grad_middle, grad_shift_mlp, grad_scale_mlp = second_back(grad_second.reshape(framed.shape))
    grad_middle = grad_middle + upstream
    grad_gate_attn = jnp.sum(grad_middle * branch, axis=1)
    grad_branch = (gate_attn * grad_middle).astype(bf16).reshape(local_len, width)
    branch_full = in_order(grad_branch, swapped(grad_branch), side)
    grad_out = tn(branch_full, attended).astype(bf16)
    grad_attended = jnp.dot(branch_full, out_whole, preferred_element_type=f32).astype(bf16)
    grad_attended, up_cuts = lax.optimization_barrier((grad_attended, up_cuts))
    up_sum = scatter_rows(up_cuts, grid, at)
    grad_qkv = attend_back(qkv, seen, frames, logs, grad_attended)
    grad_tail = jnp.concatenate([tn(first_full, grad_qkv).astype(bf16), grad_out], axis=1)
    tail_sum = scatter_rows(scatter_cut(grad_tail, grid, at), grid, at)
    qkv_sum, out_sum = tail_sum[:, : 3 * head_cols], tail_sum[:, 3 * head_cols :]
    first_other = swapped(nt(half_of(grad_qkv, 1 - side), qkv_whole).astype(bf16))
    grad_first = nt(half_of(grad_qkv, side), qkv_whole) + first_other.astype(f32)
    first_back = jax.vjp(modulated, framed, shift_attn, scale_attn)[1]
    grad_framed, grad_shift_attn, grad_scale_attn = first_back(grad_first.reshape(framed.shape))
    grad_tokens = (grad_framed + grad_middle).astype(bf16).reshape(tokens.shape)

    low = jnp.concatenate([grad_shift_attn, grad_scale_attn, grad_gate_attn[:, None]], axis=-1)
    high = jnp.concatenate([grad_shift_mlp, grad_scale_mlp, grad_gate_mlp[:, None]], axis=-1)
    low, high = low.reshape(frames_here, -1), high.reshape(frames_here, -1)
    keep = jnp.where(side == 0, low, high).astype(bf16)
    give = jnp.where(side == 0, high, low).astype(bf16)
    mine = in_order(keep, swapped(give), side)
    grad_mods = lax.all_gather(mine, "rows", axis=0, tiled=True)
    mod_sum = tn(condition_all, grad_mods)
    bias_sum = jnp.sum(grad_mods.astype(f32), axis=0)

    qkv_sum = qkv_sum.reshape(share, pairs, 3, PAIR).transpose(0, 2, 1, 3).reshape(w_qkv.shape)
    return (output, grad_tokens, qkv_sum, out_sum.T, up_sum, down_sum.T, mod_sum, bias_sum)


def solution(mesh):
    in_specs = (
        P("rows", "seq", None),
        P("rows", "seq"),
        P("rows", None),
        P("rows", None, "seq"),
        P("seq", "rows"),
        P("rows", "seq"),
        P("seq", "rows"),
        P(None, "seq"),
        P("seq"),
        P("rows", "seq", None),
    )
    out_specs = (
        P("rows", "seq", None),
        P("rows", "seq", None),
        P("rows", None, "seq"),
        P("seq", "rows"),
        P("rows", "seq"),
        P("seq", "rows"),
        P(None, "seq"),
        P("seq"),
    )
    return jax.shard_map(block, mesh=mesh, in_specs=in_specs, out_specs=out_specs, check_vma=False)
```

```python
import math

import jax
import jax.numpy as jnp
from jax import lax
from jax.experimental import pallas as pl
from jax.experimental.pallas import tpu as pltpu
from jax.sharding import PartitionSpec as P

D = 1024
HEAD = 64
FRAME = 64
PAIR = 2 * HEAD
QB = 256

norm_eps = 1e-06
hidden_score = -1e30


f32 = jnp.float32
bf16 = jnp.bfloat16


def noise_features(levels):
    half_width = D // 2
    frequency = jnp.exp(
        -math.log(10000.0) * jnp.arange(half_width).astype(jnp.float32) / half_width
    )
    angles = levels[..., None] * frequency
    return jax.nn.silu(jnp.concatenate([jnp.cos(angles), jnp.sin(angles)], axis=-1))


def normalize(values):
    centered = values - jnp.mean(values, axis=-1, keepdims=True)
    return centered * lax.rsqrt(jnp.mean(centered * centered, axis=-1, keepdims=True) + norm_eps)


def modulated(values, offsets, factors):
    return normalize(values) * (1.0 + factors) + offsets


def gelu_and_slope(values):
    square = values * values
    inner = math.sqrt(2.0 / math.pi) * (values + 0.044715 * (values * square))
    bend = jnp.tanh(inner)
    half = 0.5 * (1.0 + bend)
    steep = math.sqrt(2.0 / math.pi) * (1.0 + 3.0 * 0.044715 * square)
    slope = half + 0.5 * values * (1.0 - bend * bend) * steep
    return (values * half).astype(bf16), slope.astype(bf16)


def grid_of(count):
    deep = 4
    side = math.isqrt(count // deep)
    return (deep, side, side)


def shift_pairs(grid, axis, amount):
    pairs = []
    for z in range(grid[0]):
        for y in range(grid[1]):
            for x in range(grid[2]):
                to = [z, y, x]
                to[axis] = (to[axis] + amount) % grid[axis]
                pairs.append(
                    (
                        (z * grid[1] + y) * grid[2] + x,
                        (to[0] * grid[1] + to[1]) * grid[2] + to[2],
                    )
                )
    return pairs


def place_on(grid):
    me = lax.axis_index("rows")
    return (me // (grid[1] * grid[2]), (me // grid[2]) % grid[1], me % grid[2])


def moved(part, grid, axis, k):
    return lax.ppermute(part, "rows", shift_pairs(grid, axis, k))


def gather_axis(part, grid, axis, at, dim):
    count = grid[axis]
    whole = jnp.zeros(part.shape[:dim] + (count,) + part.shape[dim:], part.dtype)
    pieces = [part] + [moved(part, grid, axis, k) for k in range(1, count)]
    for k, piece in enumerate(pieces):
        whole = lax.dynamic_update_index_in_dim(whole, piece, (at[axis] - k) % count, dim)
    return whole


def gather_deep(shard, grid, at):
    return gather_axis(shard, grid, 0, at, 0)


def gather_rest(deep, grid, at):
    cut = deep.shape[-1] // 2
    first = gather_axis(deep[..., :cut], grid, 2, at, 1)
    first = gather_axis(first, grid, 1, at, 1)
    second = gather_axis(deep[..., cut:], grid, 1, at, 1)
    second = gather_axis(second, grid, 2, at, 2)
    whole = jnp.concatenate([first, second], axis=-1)
    return whole.reshape(-1, whole.shape[-1])


def pieces_of(whole, grid, axis, at, dim):
    return [
        lax.dynamic_index_in_dim(whole, (at[axis] + k) % grid[axis], dim, keepdims=False)
        for k in range(grid[axis])
    ]


def sum_pieces(pieces, grid, axis):
    come = [moved(pieces[k], grid, axis, k) for k in range(1, grid[axis])]
    total = pieces[0].astype(f32)
    for piece in come:
        total = total + piece.astype(f32)
    return total


def scatter_axis(whole, grid, axis, at, dim):
    return sum_pieces(pieces_of(whole, grid, axis, at, dim), grid, axis)


def scatter_cut(whole, grid, at):
    cols = whole.shape[-1]
    cut = cols // 2
    view = whole.reshape(*grid, -1, cols)
    return (
        pieces_of(view[..., :cut], grid, 1, at, 1),
        pieces_of(view[..., cut:], grid, 2, at, 2),
    )


def scatter_rows(cuts, grid, at):
    first = sum_pieces(cuts[0], grid, 1).astype(bf16)
    second = sum_pieces(cuts[1], grid, 2).astype(bf16)
    first = scatter_axis(first, grid, 2, at, 1).astype(bf16)
    second = scatter_axis(second, grid, 1, at, 1).astype(bf16)
    both = jnp.concatenate([first, second], axis=-1)
    return scatter_axis(both, grid, 0, at, 0)


def swapped(part):
    return lax.ppermute(part, "seq", [(0, 1), (1, 0)])


def in_order(own, other, side):
    whole = jnp.zeros((2 * own.shape[0],) + own.shape[1:], own.dtype)
    half = own.shape[0]
    whole = lax.dynamic_update_slice_in_dim(whole, own, side * half, 0)
    return lax.dynamic_update_slice_in_dim(whole, other, (1 - side) * half, 0)


def half_of(whole, which):
    half = whole.shape[0] // 2
    return lax.dynamic_slice_in_dim(whole, which * half, half, 0)


def nt(a, b):
    return lax.dot_general(a, b, (((1,), (1,)), ((), ())), preferred_element_type=f32)


def nn(a, b):
    return lax.dot_general(a, b, (((1,), (0,)), ((), ())), preferred_element_type=f32)


def lane_in(shape, head):
    lanes = lax.broadcasted_iota(jnp.int32, shape, 1)
    return (lanes // HEAD) == head


def forward_kernel(qkv_ref, seen_ref, frame_ref, out_ref, log_ref):
    length = qkv_ref.shape[0]
    queries = qkv_ref[:, 0:PAIR] * jnp.asarray(HEAD**-0.5, bf16)
    keys = qkv_ref[:, PAIR : 2 * PAIR]
    values_t = qkv_ref[:, 2 * PAIR : 3 * PAIR].T
    seen = seen_ref[...]
    frames = frame_ref[...]
    own = [lane_in((length, PAIR), head) for head in range(2)]
    query_h = [jnp.where(own[head], queries, seen) for head in range(2)]
    key_h = [jnp.where(own[head], keys, frames) for head in range(2)]
    for start in range(0, length, QB):
        stop = start + QB
        parts = []
        for head in range(2):
            scores = nt(key_h[head][:stop], query_h[head][start:stop])
            largest = jnp.max(scores, axis=0, keepdims=True)
            exponent = jnp.exp(scores - largest)
            denominator = jnp.sum(exponent, axis=0, keepdims=True)
            combined = nn(values_t[head * HEAD : (head + 1) * HEAD, :stop], exponent.astype(bf16))
            parts.append(combined / denominator)
            log_ref[0, head : head + 1, start:stop] = largest + jnp.log(denominator)
        out_ref[start:stop, :] = jnp.concatenate(parts, axis=0).T.astype(bf16)


def backward_kernel(qkv_ref, seen_ref, frame_ref, log_ref, grad_ref, out_ref, key_sum, value_sum):
    length = qkv_ref.shape[0]
    queries = qkv_ref[:, 0:PAIR] * jnp.asarray(HEAD**-0.5, bf16)
    keys = qkv_ref[:, PAIR : 2 * PAIR]
    values = qkv_ref[:, 2 * PAIR : 3 * PAIR]
    grads = grad_ref[...]
    keys_t = keys.T
    seen = seen_ref[...]
    frames = frame_ref[...]
    nothing = jnp.zeros((length, PAIR), bf16)
    own = [lane_in((length, PAIR), head) for head in range(2)]
    query_h = [jnp.where(own[head], queries, seen) for head in range(2)]
    query_only = [jnp.where(own[head], queries, nothing) for head in range(2)]
    key_h = [jnp.where(own[head], keys, frames) for head in range(2)]
    grad_h = [jnp.where(own[head], grads, nothing) for head in range(2)]
    for start in reversed(range(0, length, QB)):
        stop = start + QB
        query_parts = []
        for head in range(2):
            grad_block = grad_h[head][start:stop]
            scores = nt(key_h[head][:stop], query_h[head][start:stop])
            chance = jnp.exp(scores - log_ref[0, head : head + 1, start:stop])
            grad_chance = nt(values[:stop], grad_block)
            product = chance * grad_chance
            grad_scores = product - chance * jnp.sum(product, axis=0, keepdims=True)
            grad_scores = grad_scores.astype(bf16)
            value_part = nn(chance.astype(bf16), grad_block)
            key_part = nn(grad_scores, query_only[head][start:stop])
            if stop == length and head == 0:
                value_sum[...] = value_part
                key_sum[...] = key_part
            else:
                value_sum[:stop, :] += value_part
                key_sum[:stop, :] += key_part
            query_parts.append(nn(keys_t[head * HEAD : (head + 1) * HEAD, :stop], grad_scores))
        query_grad = jnp.concatenate(query_parts, axis=0).T * HEAD**-0.5
        out_ref[start:stop, 0:PAIR] = query_grad.astype(bf16)
    out_ref[:, PAIR : 2 * PAIR] = key_sum[...].astype(bf16)
    out_ref[:, 2 * PAIR : 3 * PAIR] = value_sum[...].astype(bf16)


def attend(qkv, seen, frames):
    length, cols = qkv.shape
    pairs = cols // (3 * PAIR)
    whole = pl.BlockSpec((length, PAIR), lambda p: (0, 0))
    return pl.pallas_call(
        forward_kernel,
        grid=(pairs,),
        in_specs=[pl.BlockSpec((length, 3 * PAIR), lambda p: (0, p)), whole, whole],
        out_specs=[
            pl.BlockSpec((length, PAIR), lambda p: (0, p)),
            pl.BlockSpec((1, 2, length), lambda p: (p, 0, 0)),
        ],
        out_shape=[
            jax.ShapeDtypeStruct((length, pairs * PAIR), bf16),
            jax.ShapeDtypeStruct((pairs, 2, length), f32),
        ],
        cost_estimate=pl.CostEstimate(
            flops=8 * pairs * length * length * HEAD,
            bytes_accessed=8 * pairs * length * PAIR,
            transcendentals=2 * pairs * length * length,
        ),
        name="attend",
    )(qkv, seen, frames)


def attend_back(qkv, seen, frames, logs, grads):
    length, cols = qkv.shape
    pairs = cols // (3 * PAIR)
    whole = pl.BlockSpec((length, PAIR), lambda p: (0, 0))
    return pl.pallas_call(
        backward_kernel,
        grid=(pairs,),
        in_specs=[
            pl.BlockSpec((length, 3 * PAIR), lambda p: (0, p)),
            whole,
            whole,
            pl.BlockSpec((1, 2, length), lambda p: (p, 0, 0)),
            pl.BlockSpec((length, PAIR), lambda p: (0, p)),
        ],
        out_specs=pl.BlockSpec((length, 3 * PAIR), lambda p: (0, p)),
        out_shape=jax.ShapeDtypeStruct((length, pairs * 3 * PAIR), bf16),
        scratch_shapes=[pltpu.VMEM((length, PAIR), f32), pltpu.VMEM((length, PAIR), f32)],
        cost_estimate=pl.CostEstimate(
            flops=20 * pairs * length * length * HEAD,
            bytes_accessed=14 * pairs * length * PAIR,
            transcendentals=2 * pairs * length * length,
        ),
        name="attend_back",
    )(qkv, seen, frames, logs, grads)


def frame_lanes(per_frame):
    frames = per_frame.shape[0]
    padded = jnp.pad(per_frame.astype(bf16), ((0, 0), (0, HEAD - frames)))
    return jnp.repeat(jnp.concatenate([padded, padded], axis=1), FRAME, axis=0)


def block(tokens, noise_levels, frame_clip, w_qkv, w_out, w_up, w_down, w_mod, b_mod, cotangent):
    _, local_len, width = tokens.shape
    frames_here = noise_levels.shape[1]
    grid = grid_of(lax.axis_size("rows"))
    at = place_on(grid)
    side = lax.axis_index("seq")
    share = w_qkv.shape[0]
    head_cols = w_qkv.shape[2]
    pairs = head_cols // PAIR

    qkv_share = (
        w_qkv.reshape(share, 3, pairs, PAIR).transpose(0, 2, 1, 3).reshape(share, 3 * head_cols)
    )
    levels = in_order(noise_levels[0], swapped(noise_levels[0]), side)
    condition = noise_features(levels).astype(bf16)
    condition_cols = condition.size // share
    rest_share = jnp.concatenate(
        [w_out.T, condition.reshape(share, condition_cols), w_up], axis=1
    )
    down_share = w_down.T
    qkv_deep = gather_deep(qkv_share, grid, at)
    rest_share, down_share, qkv_deep = lax.optimization_barrier(
        (rest_share, down_share, qkv_deep)
    )
    qkv_whole = gather_rest(qkv_deep, grid, at)
    down_whole = lax.all_gather(down_share, "rows", axis=0, tiled=True)
    rest_whole = gather_rest(gather_deep(rest_share, grid, at), grid, at)
    out_whole = rest_whole[:, :head_cols]
    up_whole = rest_whole[:, head_cols + condition_cols :]
    condition_all = rest_whole[:, head_cols : head_cols + condition_cols].reshape(-1, width)

    mod_cols = jnp.dot(condition, w_mod, preferred_element_type=f32) + b_mod.astype(f32)
    own_cols = half_of(mod_cols, side)
    other_cols = swapped(half_of(mod_cols, 1 - side))
    modulation = in_order(
        own_cols.reshape(frames_here, 3, width).transpose(1, 0, 2),
        other_cols.reshape(frames_here, 3, width).transpose(1, 0, 2),
        side,
    )[:, :, None]
    shift_attn, scale_attn, gate_attn, shift_mlp, scale_mlp, gate_mlp = [
        modulation[k] for k in range(6)
    ]

    framed = tokens[0].astype(f32).reshape(frames_here, FRAME, width)
    upstream = cotangent[0].astype(f32).reshape(frames_here, FRAME, width)
    first_own = modulated(framed, shift_attn, scale_attn).astype(bf16).reshape(local_len, width)
    first_full = in_order(first_own, swapped(first_own), side)
    grad_mlp = (gate_mlp * upstream).astype(bf16).reshape(local_len, width)
    grad_mlp_full = jnp.concatenate([grad_mlp, swapped(grad_mlp)], axis=0)

    clip = frame_clip[0]
    order = jnp.arange(clip.shape[0])
    visible = (clip[:, None] == clip[None, :]) & (order[None, :] <= order[:, None])
    seen = frame_lanes(jnp.where(visible, 0.0, hidden_score))
    frames = frame_lanes(jnp.eye(clip.shape[0]))

    qkv = jnp.dot(first_full, qkv_whole, preferred_element_type=f32).astype(bf16)
    attended, logs = attend(qkv, seen, frames)
    branch_other = swapped(nt(half_of(attended, 1 - side), out_whole).astype(bf16))
    branch = nt(half_of(attended, side), out_whole) + branch_other.astype(f32)
    branch = branch.reshape(framed.shape)
    middle = framed + gate_attn * branch
    second_own = modulated(middle, shift_mlp, scale_mlp).astype(bf16).reshape(local_len, width)
    second_full = jnp.concatenate([second_own, swapped(second_own)], axis=0)
    hidden_pre = jnp.dot(second_full, up_whole, preferred_element_type=f32)
    hidden, slope = lax.optimization_barrier(gelu_and_slope(hidden_pre))
    mlp_other = swapped(nt(hidden[local_len:], down_whole).astype(bf16))
    mlp_out = (nt(hidden[:local_len], down_whole) + mlp_other.astype(f32)).reshape(framed.shape)
    output = (middle + gate_mlp * mlp_out).astype(bf16).reshape(tokens.shape)
    grad_gate_mlp = jnp.sum(upstream * mlp_out, axis=1)

    def tn(a, b):
        return lax.dot_general(a, b, (((0,), (0,)), ((), ())), preferred_element_type=f32)

    grad_down = tn(grad_mlp_full, hidden).astype(bf16)
    grad_mlp_full, grad_down = lax.optimization_barrier((grad_mlp_full, grad_down))
    down_sum = lax.psum_scatter(grad_down, "rows", scatter_dimension=0, tiled=True)
    down_sum = down_sum.astype(f32)
    grad_hidden = jnp.dot(grad_mlp_full, down_whole, preferred_element_type=f32)
    grad_pre = (grad_hidden * slope.astype(f32)).astype(bf16)
    second_other = nt(grad_pre[local_len:], up_whole).astype(bf16)
    up_cuts = scatter_cut(tn(second_full, grad_pre).astype(bf16), grid, at)
    second_other, up_cuts = lax.optimization_barrier((second_other, up_cuts))
    up_sum = scatter_rows(up_cuts, grid, at)
    second_other = swapped(second_other)
    grad_second = nt(grad_pre[:local_len], up_whole) + second_other.astype(f32)
    second_back = jax.vjp(modulated, middle, shift_mlp, scale_mlp)[1]
    grad_middle, grad_shift_mlp, grad_scale_mlp = second_back(grad_second.reshape(framed.shape))
    grad_middle = grad_middle + upstream
    grad_gate_attn = jnp.sum(grad_middle * branch, axis=1)
    grad_branch = (gate_attn * grad_middle).astype(bf16).reshape(local_len, width)
    branch_full = in_order(grad_branch, swapped(grad_branch), side)
    grad_out = tn(branch_full, attended).astype(bf16)
    grad_attended = jnp.dot(branch_full, out_whole, preferred_element_type=f32).astype(bf16)
    grad_qkv = attend_back(qkv, seen, frames, logs, grad_attended)
    grad_tail = jnp.concatenate([tn(first_full, grad_qkv).astype(bf16), grad_out], axis=1)
    tail_sum = scatter_rows(scatter_cut(grad_tail, grid, at), grid, at)
    qkv_sum, out_sum = tail_sum[:, : 3 * head_cols], tail_sum[:, 3 * head_cols :]
    first_other = swapped(nt(half_of(grad_qkv, 1 - side), qkv_whole).astype(bf16))
    grad_first = nt(half_of(grad_qkv, side), qkv_whole) + first_other.astype(f32)
    first_back = jax.vjp(modulated, framed, shift_attn, scale_attn)[1]
    grad_framed, grad_shift_attn, grad_scale_attn = first_back(grad_first.reshape(framed.shape))
    grad_tokens = (grad_framed + grad_middle).astype(bf16).reshape(tokens.shape)

    low = jnp.concatenate([grad_shift_attn, grad_scale_attn, grad_gate_attn[:, None]], axis=-1)
    high = jnp.concatenate([grad_shift_mlp, grad_scale_mlp, grad_gate_mlp[:, None]], axis=-1)
    low, high = low.reshape(frames_here, -1), high.reshape(frames_here, -1)
    keep = jnp.where(side == 0, low, high).astype(bf16)
    give = jnp.where(side == 0, high, low).astype(bf16)
    give = swapped(give)
    mine = in_order(keep, give, side)
    grad_mods = gather_rest(gather_deep(mine, grid, at), grid, at)
    mod_sum = tn(condition_all, grad_mods)
    bias_sum = jnp.sum(grad_mods.astype(f32), axis=0)

    qkv_sum = qkv_sum.reshape(share, pairs, 3, PAIR).transpose(0, 2, 1, 3).reshape(w_qkv.shape)
    return (output, grad_tokens, qkv_sum, out_sum.T, up_sum, down_sum.T, mod_sum, bias_sum)


def solution(mesh):
    in_specs = (
        P("rows", "seq", None),
        P("rows", "seq"),
        P("rows", None),
        P("rows", None, "seq"),
        P("seq", "rows"),
        P("rows", "seq"),
        P("seq", "rows"),
        P(None, "seq"),
        P("seq"),
        P("rows", "seq", None),
    )
    out_specs = (
        P("rows", "seq", None),
        P("rows", "seq", None),
        P("rows", None, "seq"),
        P("seq", "rows"),
        P("rows", "seq"),
        P("seq", "rows"),
        P(None, "seq"),
        P("seq"),
    )
    return jax.shard_map(block, mesh=mesh, in_specs=in_specs, out_specs=out_specs, check_vma=False)
```

```python
import math

import jax
import jax.numpy as jnp
from jax import lax
from jax.experimental import pallas as pl
from jax.experimental.pallas import tpu as pltpu
from jax.sharding import PartitionSpec as P

D = 1024
HEAD = 64
FRAME = 64
PAIR = 2 * HEAD
QB = 256

norm_eps = 1e-06
hidden_score = -1e30


f32 = jnp.float32
bf16 = jnp.bfloat16


def noise_features(levels):
    half_width = D // 2
    frequency = jnp.exp(
        -math.log(10000.0) * jnp.arange(half_width).astype(jnp.float32) / half_width
    )
    angles = levels[..., None] * frequency
    return jax.nn.silu(jnp.concatenate([jnp.cos(angles), jnp.sin(angles)], axis=-1))


def normalize(values):
    centered = values - jnp.mean(values, axis=-1, keepdims=True)
    return centered * lax.rsqrt(jnp.mean(centered * centered, axis=-1, keepdims=True) + norm_eps)


def modulated(values, offsets, factors):
    return normalize(values) * (1.0 + factors) + offsets


def gelu_and_slope(values):
    square = values * values
    inner = math.sqrt(2.0 / math.pi) * (values + 0.044715 * (values * square))
    bend = jnp.tanh(inner)
    half = 0.5 * (1.0 + bend)
    steep = math.sqrt(2.0 / math.pi) * (1.0 + 3.0 * 0.044715 * square)
    slope = half + 0.5 * values * (1.0 - bend * bend) * steep
    return (values * half).astype(bf16), slope.astype(bf16)


def grid_of(count):
    deep = 4
    side = math.isqrt(count // deep)
    return (deep, side, side)


def shift_pairs(grid, axis, amount):
    pairs = []
    for z in range(grid[0]):
        for y in range(grid[1]):
            for x in range(grid[2]):
                to = [z, y, x]
                to[axis] = (to[axis] + amount) % grid[axis]
                pairs.append(
                    (
                        (z * grid[1] + y) * grid[2] + x,
                        (to[0] * grid[1] + to[1]) * grid[2] + to[2],
                    )
                )
    return pairs


def place_on(grid):
    me = lax.axis_index("rows")
    return (me // (grid[1] * grid[2]), (me // grid[2]) % grid[1], me % grid[2])


def moved(part, grid, axis, k):
    return lax.ppermute(part, "rows", shift_pairs(grid, axis, k))


def gather_axis(part, grid, axis, at, dim):
    count = grid[axis]
    whole = jnp.zeros(part.shape[:dim] + (count,) + part.shape[dim:], part.dtype)
    pieces = [part] + [moved(part, grid, axis, k) for k in range(1, count)]
    for k, piece in enumerate(pieces):
        whole = lax.dynamic_update_index_in_dim(whole, piece, (at[axis] - k) % count, dim)
    return whole


def gather_deep(shard, grid, at):
    return gather_axis(shard, grid, 0, at, 0)


def gather_rest(deep, grid, at):
    cut = deep.shape[-1] // 2
    first = gather_axis(deep[..., :cut], grid, 2, at, 1)
    first = gather_axis(first, grid, 1, at, 1)
    second = gather_axis(deep[..., cut:], grid, 1, at, 1)
    second = gather_axis(second, grid, 2, at, 2)
    whole = jnp.concatenate([first, second], axis=-1)
    return whole.reshape(-1, whole.shape[-1])


def pieces_of(whole, grid, axis, at, dim):
    return [
        lax.dynamic_index_in_dim(whole, (at[axis] + k) % grid[axis], dim, keepdims=False)
        for k in range(grid[axis])
    ]


def sum_pieces(pieces, grid, axis):
    come = [moved(pieces[k], grid, axis, k) for k in range(1, grid[axis])]
    total = pieces[0].astype(f32)
    for piece in come:
        total = total + piece.astype(f32)
    return total


def scatter_axis(whole, grid, axis, at, dim):
    return sum_pieces(pieces_of(whole, grid, axis, at, dim), grid, axis)


def scatter_cut(whole, grid, at):
    cols = whole.shape[-1]
    cut = cols // 2
    view = whole.reshape(*grid, -1, cols)
    return (
        pieces_of(view[..., :cut], grid, 1, at, 1),
        pieces_of(view[..., cut:], grid, 2, at, 2),
    )


def scatter_rows(cuts, grid, at):
    first = sum_pieces(cuts[0], grid, 1).astype(bf16)
    second = sum_pieces(cuts[1], grid, 2).astype(bf16)
    first = scatter_axis(first, grid, 2, at, 1).astype(bf16)
    second = scatter_axis(second, grid, 1, at, 1).astype(bf16)
    both = jnp.concatenate([first, second], axis=-1)
    return scatter_axis(both, grid, 0, at, 0)


def swapped(part):
    return lax.ppermute(part, "seq", [(0, 1), (1, 0)])


def in_order(own, other, side):
    whole = jnp.zeros((2 * own.shape[0],) + own.shape[1:], own.dtype)
    half = own.shape[0]
    whole = lax.dynamic_update_slice_in_dim(whole, own, side * half, 0)
    return lax.dynamic_update_slice_in_dim(whole, other, (1 - side) * half, 0)


def half_of(whole, which):
    half = whole.shape[0] // 2
    return lax.dynamic_slice_in_dim(whole, which * half, half, 0)


def nt(a, b):
    return lax.dot_general(a, b, (((1,), (1,)), ((), ())), preferred_element_type=f32)


def nn(a, b):
    return lax.dot_general(a, b, (((1,), (0,)), ((), ())), preferred_element_type=f32)


def lane_in(shape, head):
    lanes = lax.broadcasted_iota(jnp.int32, shape, 1)
    return (lanes // HEAD) == head


def forward_kernel(qkv_ref, seen_ref, frame_ref, out_ref, log_ref):
    length = qkv_ref.shape[0]
    queries = qkv_ref[:, 0:PAIR] * jnp.asarray(HEAD**-0.5, bf16)
    keys = qkv_ref[:, PAIR : 2 * PAIR]
    values_t = qkv_ref[:, 2 * PAIR : 3 * PAIR].T
    seen = seen_ref[...]
    frames = frame_ref[...]
    own = [lane_in((length, PAIR), head) for head in range(2)]
    query_h = [jnp.where(own[head], queries, seen) for head in range(2)]
    key_h = [jnp.where(own[head], keys, frames) for head in range(2)]
    for start in range(0, length, QB):
        stop = start + QB
        parts = []
        for head in range(2):
            scores = nt(key_h[head][:stop], query_h[head][start:stop])
            largest = jnp.max(scores, axis=0, keepdims=True)
            exponent = jnp.exp(scores - largest)
            denominator = jnp.sum(exponent, axis=0, keepdims=True)
            combined = nn(values_t[head * HEAD : (head + 1) * HEAD, :stop], exponent.astype(bf16))
            parts.append(combined / denominator)
            log_ref[0, head : head + 1, start:stop] = largest + jnp.log(denominator)
        out_ref[start:stop, :] = jnp.concatenate(parts, axis=0).T.astype(bf16)


def backward_kernel(qkv_ref, seen_ref, frame_ref, log_ref, grad_ref, *rest):
    out_ref, key_sum, value_sum = rest[-3:]
    length = qkv_ref.shape[0]
    queries = qkv_ref[:, 0:PAIR] * jnp.asarray(HEAD**-0.5, bf16)
    keys = qkv_ref[:, PAIR : 2 * PAIR]
    values = qkv_ref[:, 2 * PAIR : 3 * PAIR]
    grads = grad_ref[...]
    keys_t = keys.T
    seen = seen_ref[...]
    frames = frame_ref[...]
    nothing = jnp.zeros((length, PAIR), bf16)
    own = [lane_in((length, PAIR), head) for head in range(2)]
    query_h = [jnp.where(own[head], queries, seen) for head in range(2)]
    query_only = [jnp.where(own[head], queries, nothing) for head in range(2)]
    key_h = [jnp.where(own[head], keys, frames) for head in range(2)]
    grad_h = [jnp.where(own[head], grads, nothing) for head in range(2)]
    for start in reversed(range(0, length, QB)):
        stop = start + QB
        query_parts = []
        for head in range(2):
            grad_block = grad_h[head][start:stop]
            scores = nt(key_h[head][:stop], query_h[head][start:stop])
            chance = jnp.exp(scores - log_ref[0, head : head + 1, start:stop])
            grad_chance = nt(values[:stop], grad_block)
            product = chance * grad_chance
            grad_scores = product - chance * jnp.sum(product, axis=0, keepdims=True)
            grad_scores = grad_scores.astype(bf16)
            value_part = nn(chance.astype(bf16), grad_block)
            key_part = nn(grad_scores, query_only[head][start:stop])
            if stop == length and head == 0:
                value_sum[...] = value_part
                key_sum[...] = key_part
            else:
                value_sum[:stop, :] += value_part
                key_sum[:stop, :] += key_part
            query_parts.append(nn(keys_t[head * HEAD : (head + 1) * HEAD, :stop], grad_scores))
        query_grad = jnp.concatenate(query_parts, axis=0).T * HEAD**-0.5
        out_ref[start:stop, 0:PAIR] = query_grad.astype(bf16)
    out_ref[:, PAIR : 2 * PAIR] = key_sum[...].astype(bf16)
    out_ref[:, 2 * PAIR : 3 * PAIR] = value_sum[...].astype(bf16)


def attend(qkv, seen, frames):
    length, cols = qkv.shape
    pairs = cols // (3 * PAIR)
    whole = pl.BlockSpec((length, PAIR), lambda p: (0, 0))
    return pl.pallas_call(
        forward_kernel,
        grid=(pairs,),
        in_specs=[pl.BlockSpec((length, 3 * PAIR), lambda p: (0, p)), whole, whole],
        out_specs=[
            pl.BlockSpec((length, PAIR), lambda p: (0, p)),
            pl.BlockSpec((1, 2, length), lambda p: (p, 0, 0)),
        ],
        out_shape=[
            jax.ShapeDtypeStruct((length, pairs * PAIR), bf16),
            jax.ShapeDtypeStruct((pairs, 2, length), f32),
        ],
        cost_estimate=pl.CostEstimate(
            flops=8 * pairs * length * length * HEAD,
            bytes_accessed=8 * pairs * length * PAIR,
            transcendentals=2 * pairs * length * length,
        ),
        name="attend",
    )(qkv, seen, frames)


def attend_back(qkv, seen, frames, logs, grads, first, pairs, into=None):
    length, cols = qkv.shape
    whole = pl.BlockSpec((length, PAIR), lambda p: (0, 0))
    operands = [qkv, seen, frames, logs, grads]
    specs = [
        pl.BlockSpec((length, 3 * PAIR), lambda p: (0, p + first)),
        whole,
        whole,
        pl.BlockSpec((1, 2, length), lambda p: (p + first, 0, 0)),
        pl.BlockSpec((length, PAIR), lambda p: (0, p + first)),
    ]
    if into is not None:
        operands.append(into)
        specs.append(pl.BlockSpec(memory_space=pl.ANY))
    return pl.pallas_call(
        backward_kernel,
        grid=(pairs,),
        in_specs=specs,
        out_specs=pl.BlockSpec((length, 3 * PAIR), lambda p: (0, p + first)),
        out_shape=jax.ShapeDtypeStruct((length, cols), bf16),
        scratch_shapes=[pltpu.VMEM((length, PAIR), f32), pltpu.VMEM((length, PAIR), f32)],
        input_output_aliases={} if into is None else {5: 0},
        cost_estimate=pl.CostEstimate(
            flops=20 * pairs * length * length * HEAD,
            bytes_accessed=14 * pairs * length * PAIR,
            transcendentals=2 * pairs * length * length,
        ),
    )(*operands)


def frame_lanes(per_frame):
    frames = per_frame.shape[0]
    padded = jnp.pad(per_frame.astype(bf16), ((0, 0), (0, HEAD - frames)))
    return jnp.repeat(jnp.concatenate([padded, padded], axis=1), FRAME, axis=0)


def block(tokens, noise_levels, frame_clip, w_qkv, w_out, w_up, w_down, w_mod, b_mod, cotangent):
    _, local_len, width = tokens.shape
    frames_here = noise_levels.shape[1]
    grid = grid_of(lax.axis_size("rows"))
    at = place_on(grid)
    side = lax.axis_index("seq")
    share = w_qkv.shape[0]
    head_cols = w_qkv.shape[2]
    pairs = head_cols // PAIR
    hidden_cols = w_up.shape[1]

    qkv_share = (
        w_qkv.reshape(share, 3, pairs, PAIR).transpose(0, 2, 1, 3).reshape(share, 3 * head_cols)
    )
    qkv_share = jnp.concatenate([qkv_share, w_out.T], axis=1)
    levels = in_order(noise_levels[0], swapped(noise_levels[0]), side)
    condition = noise_features(levels).astype(bf16)
    condition_cols = condition.size // share
    rest_share = jnp.concatenate([w_up, condition.reshape(share, condition_cols)], axis=1)
    down_share = w_down.T
    qkv_deep = gather_deep(qkv_share, grid, at)
    rest_share, down_share, qkv_deep = lax.optimization_barrier(
        (rest_share, down_share, qkv_deep)
    )
    qkv_whole = gather_rest(qkv_deep, grid, at)
    down_whole = lax.all_gather(down_share, "rows", axis=0, tiled=True)
    rest_whole = gather_rest(gather_deep(rest_share, grid, at), grid, at)
    out_whole = qkv_whole[:, 3 * head_cols :]
    qkv_whole = qkv_whole[:, : 3 * head_cols]
    up_whole = rest_whole[:, :hidden_cols]
    condition_all = rest_whole[:, hidden_cols:].reshape(-1, width)

    mod_cols = jnp.dot(condition, w_mod, preferred_element_type=f32) + b_mod.astype(f32)
    own_cols = half_of(mod_cols, side)
    other_cols = swapped(half_of(mod_cols, 1 - side))
    modulation = in_order(
        own_cols.reshape(frames_here, 3, width).transpose(1, 0, 2),
        other_cols.reshape(frames_here, 3, width).transpose(1, 0, 2),
        side,
    )[:, :, None]
    shift_attn, scale_attn, gate_attn, shift_mlp, scale_mlp, gate_mlp = [
        modulation[k] for k in range(6)
    ]

    framed = tokens[0].astype(f32).reshape(frames_here, FRAME, width)
    upstream = cotangent[0].astype(f32).reshape(frames_here, FRAME, width)
    first_own = modulated(framed, shift_attn, scale_attn).astype(bf16).reshape(local_len, width)
    first_full = in_order(first_own, swapped(first_own), side)
    grad_mlp = (gate_mlp * upstream).astype(bf16).reshape(local_len, width)
    grad_mlp_full = jnp.concatenate([grad_mlp, swapped(grad_mlp)], axis=0)

    clip = frame_clip[0]
    order = jnp.arange(clip.shape[0])
    visible = (clip[:, None] == clip[None, :]) & (order[None, :] <= order[:, None])
    seen = frame_lanes(jnp.where(visible, 0.0, hidden_score))
    frames = frame_lanes(jnp.eye(clip.shape[0]))

    qkv = jnp.dot(first_full, qkv_whole, preferred_element_type=f32).astype(bf16)
    attended, logs = attend(qkv, seen, frames)
    branch_other = swapped(nt(half_of(attended, 1 - side), out_whole).astype(bf16))
    branch = nt(half_of(attended, side), out_whole) + branch_other.astype(f32)
    branch = branch.reshape(framed.shape)
    middle = framed + gate_attn * branch
    second_own = modulated(middle, shift_mlp, scale_mlp).astype(bf16).reshape(local_len, width)
    second_full = jnp.concatenate([second_own, swapped(second_own)], axis=0)
    hidden_pre = jnp.dot(second_full, up_whole, preferred_element_type=f32)
    hidden, slope = lax.optimization_barrier(gelu_and_slope(hidden_pre))
    mlp_other = swapped(nt(hidden[local_len:], down_whole).astype(bf16))
    mlp_out = (nt(hidden[:local_len], down_whole) + mlp_other.astype(f32)).reshape(framed.shape)
    output = (middle + gate_mlp * mlp_out).astype(bf16).reshape(tokens.shape)
    grad_gate_mlp = jnp.sum(upstream * mlp_out, axis=1)

    def tn(a, b):
        return lax.dot_general(a, b, (((0,), (0,)), ((), ())), preferred_element_type=f32)

    grad_down = tn(grad_mlp_full, hidden).astype(bf16)
    grad_mlp_full, grad_down = lax.optimization_barrier((grad_mlp_full, grad_down))
    down_sum = lax.psum_scatter(grad_down, "rows", scatter_dimension=0, tiled=True)
    down_sum = down_sum.astype(f32)
    grad_hidden = jnp.dot(grad_mlp_full, down_whole, preferred_element_type=f32)
    grad_pre = (grad_hidden * slope.astype(f32)).astype(bf16)
    second_other = nt(grad_pre[local_len:], up_whole).astype(bf16)
    up_cuts = scatter_cut(tn(second_full, grad_pre).astype(bf16), grid, at)
    second_other, up_cuts = lax.optimization_barrier((second_other, up_cuts))
    up_sum = scatter_rows(up_cuts, grid, at)
    second_other = swapped(second_other)
    grad_second = nt(grad_pre[:local_len], up_whole) + second_other.astype(f32)
    second_back = jax.vjp(modulated, middle, shift_mlp, scale_mlp)[1]
    grad_middle, grad_shift_mlp, grad_scale_mlp = second_back(grad_second.reshape(framed.shape))
    grad_middle = grad_middle + upstream
    grad_gate_attn = jnp.sum(grad_middle * branch, axis=1)
    grad_branch = (gate_attn * grad_middle).astype(bf16).reshape(local_len, width)
    branch_full = in_order(grad_branch, swapped(grad_branch), side)
    grad_out = tn(branch_full, attended).astype(bf16)
    grad_attended = jnp.dot(branch_full, out_whole, preferred_element_type=f32).astype(bf16)
    part = pairs // 2
    grad_qkv = attend_back(qkv, seen, frames, logs, grad_attended, 0, part)
    grad_qkv = attend_back(qkv, seen, frames, logs, grad_attended, part, pairs - part, grad_qkv)
    grad_tail = jnp.concatenate([tn(first_full, grad_qkv).astype(bf16), grad_out], axis=1)
    tail_sum = scatter_rows(scatter_cut(grad_tail, grid, at), grid, at)
    qkv_sum, out_sum = tail_sum[:, : 3 * head_cols], tail_sum[:, 3 * head_cols :]
    first_other = swapped(nt(half_of(grad_qkv, 1 - side), qkv_whole).astype(bf16))
    grad_first = nt(half_of(grad_qkv, side), qkv_whole) + first_other.astype(f32)
    first_back = jax.vjp(modulated, framed, shift_attn, scale_attn)[1]
    grad_framed, grad_shift_attn, grad_scale_attn = first_back(grad_first.reshape(framed.shape))
    grad_tokens = (grad_framed + grad_middle).astype(bf16).reshape(tokens.shape)

    low = jnp.concatenate([grad_shift_attn, grad_scale_attn, grad_gate_attn[:, None]], axis=-1)
    high = jnp.concatenate([grad_shift_mlp, grad_scale_mlp, grad_gate_mlp[:, None]], axis=-1)
    low, high = low.reshape(frames_here, -1), high.reshape(frames_here, -1)
    keep = jnp.where(side == 0, low, high).astype(bf16)
    give = jnp.where(side == 0, high, low).astype(bf16)
    give = swapped(give)
    mine = in_order(keep, give, side)
    grad_mods = gather_rest(gather_deep(mine, grid, at), grid, at)
    mod_sum = tn(condition_all, grad_mods)
    bias_sum = jnp.sum(grad_mods.astype(f32), axis=0)

    qkv_sum = qkv_sum.reshape(share, pairs, 3, PAIR).transpose(0, 2, 1, 3).reshape(w_qkv.shape)
    return (output, grad_tokens, qkv_sum, out_sum.T, up_sum, down_sum.T, mod_sum, bias_sum)


def solution(mesh):
    in_specs = (
        P("rows", "seq", None),
        P("rows", "seq"),
        P("rows", None),
        P("rows", None, "seq"),
        P("seq", "rows"),
        P("rows", "seq"),
        P("seq", "rows"),
        P(None, "seq"),
        P("seq"),
        P("rows", "seq", None),
    )
    out_specs = (
        P("rows", "seq", None),
        P("rows", "seq", None),
        P("rows", None, "seq"),
        P("seq", "rows"),
        P("rows", "seq"),
        P("seq", "rows"),
        P(None, "seq"),
        P("seq"),
    )
    return jax.shard_map(block, mesh=mesh, in_specs=in_specs, out_specs=out_specs, check_vma=False)
```

```python
import math

import jax
import jax.numpy as jnp
from jax import lax
from jax.experimental import pallas as pl
from jax.experimental.pallas import tpu as pltpu
from jax.sharding import PartitionSpec as P

D = 1024
HEAD = 64
FRAME = 64
PAIR = 2 * HEAD
QB = 256

norm_eps = 1e-06
hidden_score = -1e30


f32 = jnp.float32
bf16 = jnp.bfloat16


def noise_features(levels):
    half_width = D // 2
    frequency = jnp.exp(
        -math.log(10000.0) * jnp.arange(half_width).astype(jnp.float32) / half_width
    )
    angles = levels[..., None] * frequency
    return jax.nn.silu(jnp.concatenate([jnp.cos(angles), jnp.sin(angles)], axis=-1))


def normalize(values):
    centered = values - jnp.mean(values, axis=-1, keepdims=True)
    return centered * lax.rsqrt(jnp.mean(centered * centered, axis=-1, keepdims=True) + norm_eps)


def modulated(values, offsets, factors):
    return normalize(values) * (1.0 + factors) + offsets


def gelu_and_slope(values):
    square = values * values
    inner = math.sqrt(2.0 / math.pi) * (values + 0.044715 * (values * square))
    bend = jnp.tanh(inner)
    half = 0.5 * (1.0 + bend)
    steep = math.sqrt(2.0 / math.pi) * (1.0 + 3.0 * 0.044715 * square)
    slope = half + 0.5 * values * (1.0 - bend * bend) * steep
    return (values * half).astype(bf16), slope.astype(bf16)


def grid_of(count):
    deep = 4
    side = math.isqrt(count // deep)
    return (deep, side, side)


def shift_pairs(grid, axis, amount):
    pairs = []
    for z in range(grid[0]):
        for y in range(grid[1]):
            for x in range(grid[2]):
                to = [z, y, x]
                to[axis] = (to[axis] + amount) % grid[axis]
                pairs.append(
                    (
                        (z * grid[1] + y) * grid[2] + x,
                        (to[0] * grid[1] + to[1]) * grid[2] + to[2],
                    )
                )
    return pairs


def place_on(grid):
    me = lax.axis_index("rows")
    return (me // (grid[1] * grid[2]), (me // grid[2]) % grid[1], me % grid[2])


def moved(part, grid, axis, k):
    return lax.ppermute(part, "rows", shift_pairs(grid, axis, k))


def gather_axis(part, grid, axis, at, dim):
    count = grid[axis]
    whole = jnp.zeros(part.shape[:dim] + (count,) + part.shape[dim:], part.dtype)
    pieces = [part] + [moved(part, grid, axis, k) for k in range(1, count)]
    for k, piece in enumerate(pieces):
        whole = lax.dynamic_update_index_in_dim(whole, piece, (at[axis] - k) % count, dim)
    return whole


def gather_deep(shard, grid, at):
    return gather_axis(shard, grid, 0, at, 0)


def gather_rest(deep, grid, at):
    cut = deep.shape[-1] // 2
    first = gather_axis(deep[..., :cut], grid, 2, at, 1)
    first = gather_axis(first, grid, 1, at, 1)
    second = gather_axis(deep[..., cut:], grid, 1, at, 1)
    second = gather_axis(second, grid, 2, at, 2)
    whole = jnp.concatenate([first, second], axis=-1)
    return whole.reshape(-1, whole.shape[-1])


def pieces_of(whole, grid, axis, at, dim):
    return [
        lax.dynamic_index_in_dim(whole, (at[axis] + k) % grid[axis], dim, keepdims=False)
        for k in range(grid[axis])
    ]


def sum_pieces(pieces, grid, axis, kept=bf16):
    come = [moved(pieces[k], grid, axis, k) for k in range(1, grid[axis])]
    total = pieces[0].astype(f32)
    for piece in come:
        total = total + piece.astype(f32)
    return total.astype(kept)


def scatter_axis(whole, grid, axis, at, dim, kept=bf16):
    return sum_pieces(pieces_of(whole, grid, axis, at, dim), grid, axis, kept)


def scatter_cut(whole, grid, at):
    cols = whole.shape[-1]
    cut = cols // 2
    view = whole.reshape(*grid, -1, cols)
    return (
        pieces_of(view[..., :cut], grid, 1, at, 1),
        pieces_of(view[..., cut:], grid, 2, at, 2),
    )


def scatter_rows(cuts, grid, at):
    first = sum_pieces(cuts[0], grid, 1)
    second = sum_pieces(cuts[1], grid, 2)
    first = scatter_axis(first, grid, 2, at, 1)
    second = scatter_axis(second, grid, 1, at, 1)
    both = jnp.concatenate([first, second], axis=-1)
    return scatter_axis(both, grid, 0, at, 0, f32)


def swapped(part):
    return lax.ppermute(part, "seq", [(0, 1), (1, 0)])


def in_order(own, other, side):
    whole = jnp.zeros((2 * own.shape[0],) + own.shape[1:], own.dtype)
    half = own.shape[0]
    whole = lax.dynamic_update_slice_in_dim(whole, own, side * half, 0)
    return lax.dynamic_update_slice_in_dim(whole, other, (1 - side) * half, 0)


def half_of(whole, which):
    half = whole.shape[0] // 2
    return lax.dynamic_slice_in_dim(whole, which * half, half, 0)


def nt(a, b):
    return lax.dot_general(a, b, (((1,), (1,)), ((), ())), preferred_element_type=f32)


def nn(a, b):
    return lax.dot_general(a, b, (((1,), (0,)), ((), ())), preferred_element_type=f32)


def lane_in(shape, head):
    lanes = lax.broadcasted_iota(jnp.int32, shape, 1)
    return (lanes // HEAD) == head


def forward_kernel(qkv_ref, seen_ref, frame_ref, *rest):
    out_ref, log_ref = rest[-2:]
    length = qkv_ref.shape[0]
    queries = qkv_ref[:, 0:PAIR] * jnp.asarray(HEAD**-0.5, bf16)
    keys = qkv_ref[:, PAIR : 2 * PAIR]
    values_t = qkv_ref[:, 2 * PAIR : 3 * PAIR].T
    seen = seen_ref[...]
    frames = frame_ref[...]
    own = [lane_in((length, PAIR), head) for head in range(2)]
    query_h = [jnp.where(own[head], queries, seen) for head in range(2)]
    key_h = [jnp.where(own[head], keys, frames) for head in range(2)]
    for start in range(0, length, QB):
        stop = start + QB
        parts = []
        for head in range(2):
            scores = nt(key_h[head][:stop], query_h[head][start:stop])
            largest = jnp.max(scores, axis=0, keepdims=True)
            exponent = jnp.exp(scores - largest)
            denominator = jnp.sum(exponent, axis=0, keepdims=True)
            combined = nn(values_t[head * HEAD : (head + 1) * HEAD, :stop], exponent.astype(bf16))
            parts.append(combined / denominator)
            log_ref[0, head : head + 1, start:stop] = largest + jnp.log(denominator)
        out_ref[start:stop, :] = jnp.concatenate(parts, axis=0).T.astype(bf16)


def backward_kernel(qkv_ref, seen_ref, frame_ref, log_ref, grad_ref, *rest):
    out_ref, key_sum, value_sum = rest[-3:]
    length = qkv_ref.shape[0]
    queries = qkv_ref[:, 0:PAIR] * jnp.asarray(HEAD**-0.5, bf16)
    keys = qkv_ref[:, PAIR : 2 * PAIR]
    values = qkv_ref[:, 2 * PAIR : 3 * PAIR]
    grads = grad_ref[...]
    keys_t = keys.T
    seen = seen_ref[...]
    frames = frame_ref[...]
    nothing = jnp.zeros((length, PAIR), bf16)
    own = [lane_in((length, PAIR), head) for head in range(2)]
    query_h = [jnp.where(own[head], queries, seen) for head in range(2)]
    query_only = [jnp.where(own[head], queries, nothing) for head in range(2)]
    key_h = [jnp.where(own[head], keys, frames) for head in range(2)]
    grad_h = [jnp.where(own[head], grads, nothing) for head in range(2)]
    for start in reversed(range(0, length, QB)):
        stop = start + QB
        query_parts = []
        for head in range(2):
            grad_block = grad_h[head][start:stop]
            scores = nt(key_h[head][:stop], query_h[head][start:stop])
            chance = jnp.exp(scores - log_ref[0, head : head + 1, start:stop])
            grad_chance = nt(values[:stop], grad_block)
            product = chance * grad_chance
            grad_scores = product - chance * jnp.sum(product, axis=0, keepdims=True)
            grad_scores = grad_scores.astype(bf16)
            value_part = nn(chance.astype(bf16), grad_block)
            key_part = nn(grad_scores, query_only[head][start:stop])
            if stop == length and head == 0:
                value_sum[...] = value_part
                key_sum[...] = key_part
            else:
                value_sum[:stop, :] += value_part
                key_sum[:stop, :] += key_part
            query_parts.append(nn(keys_t[head * HEAD : (head + 1) * HEAD, :stop], grad_scores))
        query_grad = jnp.concatenate(query_parts, axis=0).T * HEAD**-0.5
        out_ref[start:stop, 0:PAIR] = query_grad.astype(bf16)
    out_ref[:, PAIR : 2 * PAIR] = key_sum[...].astype(bf16)
    out_ref[:, 2 * PAIR : 3 * PAIR] = value_sum[...].astype(bf16)


def attend(qkv, seen, frames, first, pairs, into=()):
    length, cols = qkv.shape
    every = cols // (3 * PAIR)
    whole = pl.BlockSpec((length, PAIR), lambda p: (0, 0))
    return pl.pallas_call(
        forward_kernel,
        grid=(pairs,),
        in_specs=[pl.BlockSpec((length, 3 * PAIR), lambda p: (0, p + first)), whole, whole]
        + [pl.BlockSpec(memory_space=pl.ANY) for _ in into],
        out_specs=[
            pl.BlockSpec((length, PAIR), lambda p: (0, p + first)),
            pl.BlockSpec((1, 2, length), lambda p: (p + first, 0, 0)),
        ],
        out_shape=[
            jax.ShapeDtypeStruct((length, every * PAIR), bf16),
            jax.ShapeDtypeStruct((every, 2, length), f32),
        ],
        input_output_aliases={3 + k: k for k in range(len(into))},
        cost_estimate=pl.CostEstimate(
            flops=8 * pairs * length * length * HEAD,
            bytes_accessed=8 * pairs * length * PAIR,
            transcendentals=2 * pairs * length * length,
        ),
    )(qkv, seen, frames, *into)


def attend_back(qkv, seen, frames, logs, grads, first, pairs, into=None):
    length, cols = qkv.shape
    whole = pl.BlockSpec((length, PAIR), lambda p: (0, 0))
    operands = [qkv, seen, frames, logs, grads]
    specs = [
        pl.BlockSpec((length, 3 * PAIR), lambda p: (0, p + first)),
        whole,
        whole,
        pl.BlockSpec((1, 2, length), lambda p: (p + first, 0, 0)),
        pl.BlockSpec((length, PAIR), lambda p: (0, p + first)),
    ]
    if into is not None:
        operands.append(into)
        specs.append(pl.BlockSpec(memory_space=pl.ANY))
    return pl.pallas_call(
        backward_kernel,
        grid=(pairs,),
        in_specs=specs,
        out_specs=pl.BlockSpec((length, 3 * PAIR), lambda p: (0, p + first)),
        out_shape=jax.ShapeDtypeStruct((length, cols), bf16),
        scratch_shapes=[pltpu.VMEM((length, PAIR), f32), pltpu.VMEM((length, PAIR), f32)],
        input_output_aliases={} if into is None else {5: 0},
        cost_estimate=pl.CostEstimate(
            flops=20 * pairs * length * length * HEAD,
            bytes_accessed=14 * pairs * length * PAIR,
            transcendentals=2 * pairs * length * length,
        ),
    )(*operands)


def frame_lanes(per_frame):
    frames = per_frame.shape[0]
    padded = jnp.pad(per_frame.astype(bf16), ((0, 0), (0, HEAD - frames)))
    return jnp.repeat(jnp.concatenate([padded, padded], axis=1), FRAME, axis=0)


def block(tokens, noise_levels, frame_clip, w_qkv, w_out, w_up, w_down, w_mod, b_mod, cotangent):
    _, local_len, width = tokens.shape
    frames_here = noise_levels.shape[1]
    grid = grid_of(lax.axis_size("rows"))
    at = place_on(grid)
    side = lax.axis_index("seq")
    share = w_qkv.shape[0]
    head_cols = w_qkv.shape[2]
    pairs = head_cols // PAIR
    hidden_cols = w_up.shape[1]

    qkv_share = (
        w_qkv.reshape(share, 3, pairs, PAIR).transpose(0, 2, 1, 3).reshape(share, 3 * head_cols)
    )
    qkv_share = jnp.concatenate([qkv_share, w_out.T], axis=1)
    levels = in_order(noise_levels[0], swapped(noise_levels[0]), side)
    condition = noise_features(levels).astype(bf16)
    condition_cols = condition.size // share
    rest_share = jnp.concatenate([w_up, condition.reshape(share, condition_cols)], axis=1)
    down_share = w_down.T
    qkv_deep = gather_deep(qkv_share, grid, at)
    rest_share, qkv_deep = lax.optimization_barrier((rest_share, qkv_deep))
    qkv_whole = gather_rest(qkv_deep, grid, at)
    down_whole = lax.all_gather(down_share, "rows", axis=0, tiled=True)
    rest_whole = gather_rest(gather_deep(rest_share, grid, at), grid, at)
    out_whole = qkv_whole[:, 3 * head_cols :]
    qkv_whole = qkv_whole[:, : 3 * head_cols]
    up_whole = rest_whole[:, :hidden_cols]
    condition_all = rest_whole[:, hidden_cols:].reshape(-1, width)

    mod_cols = jnp.dot(condition, w_mod, preferred_element_type=f32) + b_mod.astype(f32)
    own_cols = half_of(mod_cols, side)
    other_cols = swapped(half_of(mod_cols, 1 - side))
    modulation = in_order(
        own_cols.reshape(frames_here, 3, width).transpose(1, 0, 2),
        other_cols.reshape(frames_here, 3, width).transpose(1, 0, 2),
        side,
    )[:, :, None]
    shift_attn, scale_attn, gate_attn, shift_mlp, scale_mlp, gate_mlp = [
        modulation[k] for k in range(6)
    ]

    framed = tokens[0].astype(f32).reshape(frames_here, FRAME, width)
    upstream = cotangent[0].astype(f32).reshape(frames_here, FRAME, width)
    first_own = modulated(framed, shift_attn, scale_attn).astype(bf16).reshape(local_len, width)
    first_full = in_order(first_own, swapped(first_own), side)
    grad_mlp = (gate_mlp * upstream).astype(bf16).reshape(local_len, width)
    grad_mlp_full = jnp.concatenate([grad_mlp, swapped(grad_mlp)], axis=0)

    clip = frame_clip[0]
    order = jnp.arange(clip.shape[0])
    visible = (clip[:, None] == clip[None, :]) & (order[None, :] <= order[:, None])
    seen = frame_lanes(jnp.where(visible, 0.0, hidden_score))
    frames = frame_lanes(jnp.eye(clip.shape[0]))

    qkv = jnp.dot(first_full, qkv_whole, preferred_element_type=f32).astype(bf16)
    part = pairs // 2
    into = attend(qkv, seen, frames, 0, part)
    attended, logs = attend(qkv, seen, frames, part, pairs - part, into)
    branch_other = swapped(nt(half_of(attended, 1 - side), out_whole).astype(bf16))
    branch = nt(half_of(attended, side), out_whole) + branch_other.astype(f32)
    branch = branch.reshape(framed.shape)
    middle = framed + gate_attn * branch
    second_own = modulated(middle, shift_mlp, scale_mlp).astype(bf16).reshape(local_len, width)
    second_full = jnp.concatenate([second_own, swapped(second_own)], axis=0)
    hidden_pre = jnp.dot(second_full, up_whole, preferred_element_type=f32)
    hidden, slope = lax.optimization_barrier(gelu_and_slope(hidden_pre))
    mlp_other = swapped(nt(hidden[local_len:], down_whole).astype(bf16))
    mlp_out = (nt(hidden[:local_len], down_whole) + mlp_other.astype(f32)).reshape(framed.shape)
    output = (middle + gate_mlp * mlp_out).astype(bf16).reshape(tokens.shape)
    grad_gate_mlp = jnp.sum(upstream * mlp_out, axis=1)

    def tn(a, b):
        return lax.dot_general(a, b, (((0,), (0,)), ((), ())), preferred_element_type=f32)

    grad_down = tn(grad_mlp_full, hidden).astype(bf16)
    grad_mlp_full, grad_down = lax.optimization_barrier((grad_mlp_full, grad_down))
    down_sum = lax.psum_scatter(grad_down, "rows", scatter_dimension=0, tiled=True)
    down_sum = down_sum.astype(f32)
    grad_hidden = jnp.dot(grad_mlp_full, down_whole, preferred_element_type=f32)
    grad_pre = (grad_hidden * slope.astype(f32)).astype(bf16)
    second_other = nt(grad_pre[local_len:], up_whole).astype(bf16)
    up_cuts = scatter_cut(tn(second_full, grad_pre).astype(bf16), grid, at)
    second_other, up_cuts = lax.optimization_barrier((second_other, up_cuts))
    up_sum = scatter_rows(up_cuts, grid, at)
    second_other = swapped(second_other)
    grad_second = nt(grad_pre[:local_len], up_whole) + second_other.astype(f32)
    second_back = jax.vjp(modulated, middle, shift_mlp, scale_mlp)[1]
    grad_middle, grad_shift_mlp, grad_scale_mlp = second_back(grad_second.reshape(framed.shape))
    grad_middle = grad_middle + upstream
    grad_gate_attn = jnp.sum(grad_middle * branch, axis=1)
    grad_branch = (gate_attn * grad_middle).astype(bf16).reshape(local_len, width)
    branch_full = in_order(grad_branch, swapped(grad_branch), side)
    grad_out = tn(branch_full, attended).astype(bf16)
    grad_attended = jnp.dot(branch_full, out_whole, preferred_element_type=f32).astype(bf16)
    grad_qkv = attend_back(qkv, seen, frames, logs, grad_attended, 0, part)
    grad_qkv = attend_back(qkv, seen, frames, logs, grad_attended, part, pairs - part, grad_qkv)
    grad_tail = jnp.concatenate([tn(first_full, grad_qkv).astype(bf16), grad_out], axis=1)
    tail_sum = scatter_rows(scatter_cut(grad_tail, grid, at), grid, at)
    qkv_sum, out_sum = tail_sum[:, : 3 * head_cols], tail_sum[:, 3 * head_cols :]
    first_other = swapped(nt(half_of(grad_qkv, 1 - side), qkv_whole).astype(bf16))
    grad_first = nt(half_of(grad_qkv, side), qkv_whole) + first_other.astype(f32)
    first_back = jax.vjp(modulated, framed, shift_attn, scale_attn)[1]
    grad_framed, grad_shift_attn, grad_scale_attn = first_back(grad_first.reshape(framed.shape))
    grad_tokens = (grad_framed + grad_middle).astype(bf16).reshape(tokens.shape)

    low = jnp.concatenate([grad_shift_attn, grad_scale_attn, grad_gate_attn[:, None]], axis=-1)
    high = jnp.concatenate([grad_shift_mlp, grad_scale_mlp, grad_gate_mlp[:, None]], axis=-1)
    low, high = low.reshape(frames_here, -1), high.reshape(frames_here, -1)
    keep = jnp.where(side == 0, low, high).astype(bf16)
    give = jnp.where(side == 0, high, low).astype(bf16)
    give = swapped(give)
    mine = in_order(keep, give, side)
    grad_mods = gather_rest(gather_deep(mine, grid, at), grid, at)
    mod_sum = tn(condition_all, grad_mods)
    bias_sum = jnp.sum(grad_mods.astype(f32), axis=0)

    qkv_sum = qkv_sum.reshape(share, pairs, 3, PAIR).transpose(0, 2, 1, 3).reshape(w_qkv.shape)
    return (output, grad_tokens, qkv_sum, out_sum.T, up_sum, down_sum.T, mod_sum, bias_sum)


def solution(mesh):
    in_specs = (
        P("rows", "seq", None),
        P("rows", "seq"),
        P("rows", None),
        P("rows", None, "seq"),
        P("seq", "rows"),
        P("rows", "seq"),
        P("seq", "rows"),
        P(None, "seq"),
        P("seq"),
        P("rows", "seq", None),
    )
    out_specs = (
        P("rows", "seq", None),
        P("rows", "seq", None),
        P("rows", None, "seq"),
        P("seq", "rows"),
        P("rows", "seq"),
        P("seq", "rows"),
        P(None, "seq"),
        P("seq"),
    )
    return jax.shard_map(block, mesh=mesh, in_specs=in_specs, out_specs=out_specs, check_vma=False)
```

```python
import math

import jax
import jax.numpy as jnp
from jax import lax
from jax.experimental import pallas as pl
from jax.experimental.pallas import tpu as pltpu
from jax.sharding import PartitionSpec as P

D = 1024
HEAD = 64
FRAME = 64
PAIR = 2 * HEAD
QB = 256

norm_eps = 1e-06
hidden_score = -1e30


f32 = jnp.float32
bf16 = jnp.bfloat16


def noise_features(levels):
    half_width = D // 2
    frequency = jnp.exp(
        -math.log(10000.0) * jnp.arange(half_width).astype(jnp.float32) / half_width
    )
    angles = levels[..., None] * frequency
    return jax.nn.silu(jnp.concatenate([jnp.cos(angles), jnp.sin(angles)], axis=-1))


def normalize(values):
    centered = values - jnp.mean(values, axis=-1, keepdims=True)
    return centered * lax.rsqrt(jnp.mean(centered * centered, axis=-1, keepdims=True) + norm_eps)


def modulated(values, offsets, factors):
    return normalize(values) * (1.0 + factors) + offsets


def gelu_and_slope(values):
    square = values * values
    inner = math.sqrt(2.0 / math.pi) * (values + 0.044715 * (values * square))
    bend = jnp.tanh(inner)
    half = 0.5 * (1.0 + bend)
    steep = math.sqrt(2.0 / math.pi) * (1.0 + 3.0 * 0.044715 * square)
    slope = half + 0.5 * values * (1.0 - bend * bend) * steep
    return (values * half).astype(bf16), slope.astype(bf16)


def grid_of(count):
    deep = 4
    side = math.isqrt(count // deep)
    return (deep, side, side)


def shift_pairs(grid, axis, amount):
    pairs = []
    for z in range(grid[0]):
        for y in range(grid[1]):
            for x in range(grid[2]):
                to = [z, y, x]
                to[axis] = (to[axis] + amount) % grid[axis]
                pairs.append(
                    (
                        (z * grid[1] + y) * grid[2] + x,
                        (to[0] * grid[1] + to[1]) * grid[2] + to[2],
                    )
                )
    return pairs


def place_on(grid):
    me = lax.axis_index("rows")
    return (me // (grid[1] * grid[2]), (me // grid[2]) % grid[1], me % grid[2])


def moved(part, grid, axis, k):
    return lax.ppermute(part, "rows", shift_pairs(grid, axis, k))


def gather_axis(part, grid, axis, at, dim):
    count = grid[axis]
    whole = jnp.zeros(part.shape[:dim] + (count,) + part.shape[dim:], part.dtype)
    pieces = [part] + [moved(part, grid, axis, k) for k in range(1, count)]
    for k, piece in enumerate(pieces):
        whole = lax.dynamic_update_index_in_dim(whole, piece, (at[axis] - k) % count, dim)
    return whole


def gather_deep(shard, grid, at):
    return gather_axis(shard, grid, 0, at, 0)


def gather_rest(deep, grid, at):
    cut = deep.shape[-1] // 2
    first = gather_axis(deep[..., :cut], grid, 2, at, 1)
    first = gather_axis(first, grid, 1, at, 1)
    second = gather_axis(deep[..., cut:], grid, 1, at, 1)
    second = gather_axis(second, grid, 2, at, 2)
    whole = jnp.concatenate([first, second], axis=-1)
    return whole.reshape(-1, whole.shape[-1])


def pieces_of(whole, grid, axis, at, dim):
    return [
        lax.dynamic_index_in_dim(whole, (at[axis] + k) % grid[axis], dim, keepdims=False)
        for k in range(grid[axis])
    ]


def sum_pieces(pieces, grid, axis, kept=bf16):
    come = [moved(pieces[k], grid, axis, k) for k in range(1, grid[axis])]
    total = pieces[0].astype(f32)
    for piece in come:
        total = total + piece.astype(f32)
    return total.astype(kept)


def scatter_axis(whole, grid, axis, at, dim, kept=bf16):
    return sum_pieces(pieces_of(whole, grid, axis, at, dim), grid, axis, kept)


def scatter_cut(whole, grid, at):
    cols = whole.shape[-1]
    cut = cols // 2
    view = whole.reshape(*grid, -1, cols)
    return (
        pieces_of(view[..., :cut], grid, 1, at, 1),
        pieces_of(view[..., cut:], grid, 2, at, 2),
    )


def scatter_rows(cuts, grid, at):
    first = sum_pieces(cuts[0], grid, 1)
    second = sum_pieces(cuts[1], grid, 2)
    first = scatter_axis(first, grid, 2, at, 1)
    second = scatter_axis(second, grid, 1, at, 1)
    both = jnp.concatenate([first, second], axis=-1)
    return scatter_axis(both, grid, 0, at, 0, f32)


def swapped(part):
    return lax.ppermute(part, "seq", [(0, 1), (1, 0)])


def in_order(own, other, side):
    whole = jnp.zeros((2 * own.shape[0],) + own.shape[1:], own.dtype)
    half = own.shape[0]
    whole = lax.dynamic_update_slice_in_dim(whole, own, side * half, 0)
    return lax.dynamic_update_slice_in_dim(whole, other, (1 - side) * half, 0)


def half_of(whole, which):
    half = whole.shape[0] // 2
    return lax.dynamic_slice_in_dim(whole, which * half, half, 0)


def nt(a, b):
    return lax.dot_general(a, b, (((1,), (1,)), ((), ())), preferred_element_type=f32)


def nn(a, b):
    return lax.dot_general(a, b, (((1,), (0,)), ((), ())), preferred_element_type=f32)


def lane_in(shape, head):
    lanes = lax.broadcasted_iota(jnp.int32, shape, 1)
    return (lanes // HEAD) == head


def forward_kernel(qkv_ref, seen_ref, frame_ref, *rest):
    out_ref, log_ref = rest[-2:]
    length = qkv_ref.shape[0]
    queries = qkv_ref[:, 0:PAIR] * jnp.asarray(HEAD**-0.5, bf16)
    keys = qkv_ref[:, PAIR : 2 * PAIR]
    values_t = qkv_ref[:, 2 * PAIR : 3 * PAIR].T
    seen = seen_ref[...]
    frames = frame_ref[...]
    own = [lane_in((length, PAIR), head) for head in range(2)]
    query_h = [jnp.where(own[head], queries, seen) for head in range(2)]
    key_h = [jnp.where(own[head], keys, frames) for head in range(2)]
    for start in range(0, length, QB):
        stop = start + QB
        parts = []
        for head in range(2):
            scores = nt(key_h[head][:stop], query_h[head][start:stop])
            largest = jnp.max(scores, axis=0, keepdims=True)
            exponent = jnp.exp(scores - largest)
            denominator = jnp.sum(exponent, axis=0, keepdims=True)
            combined = nn(values_t[head * HEAD : (head + 1) * HEAD, :stop], exponent.astype(bf16))
            parts.append(combined / denominator)
            log_ref[0, head : head + 1, start:stop] = largest + jnp.log(denominator)
        out_ref[start:stop, :] = jnp.concatenate(parts, axis=0).T.astype(bf16)


def backward_kernel(qkv_ref, seen_ref, frame_ref, log_ref, grad_ref, *rest):
    out_ref, key_sum, value_sum = rest[-3:]
    length = qkv_ref.shape[0]
    queries = qkv_ref[:, 0:PAIR] * jnp.asarray(HEAD**-0.5, bf16)
    keys = qkv_ref[:, PAIR : 2 * PAIR]
    values = qkv_ref[:, 2 * PAIR : 3 * PAIR]
    grads = grad_ref[...]
    keys_t = keys.T
    seen = seen_ref[...]
    frames = frame_ref[...]
    nothing = jnp.zeros((length, PAIR), bf16)
    own = [lane_in((length, PAIR), head) for head in range(2)]
    query_h = [jnp.where(own[head], queries, seen) for head in range(2)]
    query_only = [jnp.where(own[head], queries, nothing) for head in range(2)]
    key_h = [jnp.where(own[head], keys, frames) for head in range(2)]
    grad_h = [jnp.where(own[head], grads, nothing) for head in range(2)]
    for start in reversed(range(0, length, QB)):
        stop = start + QB
        query_parts = []
        for head in range(2):
            grad_block = grad_h[head][start:stop]
            scores = nt(key_h[head][:stop], query_h[head][start:stop])
            chance = jnp.exp(scores - log_ref[0, head : head + 1, start:stop])
            grad_chance = nt(values[:stop], grad_block)
            product = chance * grad_chance
            grad_scores = product - chance * jnp.sum(product, axis=0, keepdims=True)
            grad_scores = grad_scores.astype(bf16)
            value_part = nn(chance.astype(bf16), grad_block)
            key_part = nn(grad_scores, query_only[head][start:stop])
            if stop == length and head == 0:
                value_sum[...] = value_part
                key_sum[...] = key_part
            else:
                value_sum[:stop, :] += value_part
                key_sum[:stop, :] += key_part
            query_parts.append(nn(keys_t[head * HEAD : (head + 1) * HEAD, :stop], grad_scores))
        query_grad = jnp.concatenate(query_parts, axis=0).T * HEAD**-0.5
        out_ref[start:stop, 0:PAIR] = query_grad.astype(bf16)
    out_ref[:, PAIR : 2 * PAIR] = key_sum[...].astype(bf16)
    out_ref[:, 2 * PAIR : 3 * PAIR] = value_sum[...].astype(bf16)


def attend(qkv, seen, frames, first, pairs, into=()):
    length, cols = qkv.shape
    every = cols // (3 * PAIR)
    whole = pl.BlockSpec((length, PAIR), lambda p: (0, 0))
    return pl.pallas_call(
        forward_kernel,
        grid=(pairs,),
        in_specs=[pl.BlockSpec((length, 3 * PAIR), lambda p: (0, p + first)), whole, whole]
        + [pl.BlockSpec(memory_space=pl.ANY) for _ in into],
        out_specs=[
            pl.BlockSpec((length, PAIR), lambda p: (0, p + first)),
            pl.BlockSpec((1, 2, length), lambda p: (p + first, 0, 0)),
        ],
        out_shape=[
            jax.ShapeDtypeStruct((length, every * PAIR), bf16),
            jax.ShapeDtypeStruct((every, 2, length), f32),
        ],
        input_output_aliases={3 + k: k for k in range(len(into))},
        cost_estimate=pl.CostEstimate(
            flops=8 * pairs * length * length * HEAD,
            bytes_accessed=8 * pairs * length * PAIR,
            transcendentals=2 * pairs * length * length,
        ),
    )(qkv, seen, frames, *into)


def attend_back(qkv, seen, frames, logs, grads, first, pairs, into=None):
    length, cols = qkv.shape
    whole = pl.BlockSpec((length, PAIR), lambda p: (0, 0))
    operands = [qkv, seen, frames, logs, grads]
    specs = [
        pl.BlockSpec((length, 3 * PAIR), lambda p: (0, p + first)),
        whole,
        whole,
        pl.BlockSpec((1, 2, length), lambda p: (p + first, 0, 0)),
        pl.BlockSpec((length, PAIR), lambda p: (0, p + first)),
    ]
    if into is not None:
        operands.append(into)
        specs.append(pl.BlockSpec(memory_space=pl.ANY))
    return pl.pallas_call(
        backward_kernel,
        grid=(pairs,),
        in_specs=specs,
        out_specs=pl.BlockSpec((length, 3 * PAIR), lambda p: (0, p + first)),
        out_shape=jax.ShapeDtypeStruct((length, cols), bf16),
        scratch_shapes=[pltpu.VMEM((length, PAIR), f32), pltpu.VMEM((length, PAIR), f32)],
        input_output_aliases={} if into is None else {5: 0},
        cost_estimate=pl.CostEstimate(
            flops=20 * pairs * length * length * HEAD,
            bytes_accessed=14 * pairs * length * PAIR,
            transcendentals=2 * pairs * length * length,
        ),
    )(*operands)


def frame_lanes(per_frame):
    frames = per_frame.shape[0]
    padded = jnp.pad(per_frame.astype(bf16), ((0, 0), (0, HEAD - frames)))
    return jnp.repeat(jnp.concatenate([padded, padded], axis=1), FRAME, axis=0)


def block(tokens, noise_levels, frame_clip, w_qkv, w_out, w_up, w_down, w_mod, b_mod, cotangent):
    _, local_len, width = tokens.shape
    frames_here = noise_levels.shape[1]
    grid = grid_of(lax.axis_size("rows"))
    at = place_on(grid)
    side = lax.axis_index("seq")
    share = w_qkv.shape[0]
    head_cols = w_qkv.shape[2]
    pairs = head_cols // PAIR
    hidden_cols = w_up.shape[1]

    qkv_share = (
        w_qkv.reshape(share, 3, pairs, PAIR).transpose(0, 2, 1, 3).reshape(share, 3 * head_cols)
    )
    qkv_share = jnp.concatenate([qkv_share, w_out.T], axis=1)
    levels = in_order(noise_levels[0], swapped(noise_levels[0]), side)
    condition = noise_features(levels).astype(bf16)
    condition_cols = condition.size // share
    rest_share = jnp.concatenate([w_up, condition.reshape(share, condition_cols)], axis=1)
    down_share = w_down.T
    qkv_deep = gather_deep(qkv_share, grid, at)
    rest_share, qkv_deep = lax.optimization_barrier((rest_share, qkv_deep))
    qkv_whole = gather_rest(qkv_deep, grid, at)
    down_whole = lax.all_gather(down_share, "rows", axis=0, tiled=True)
    rest_whole = gather_rest(gather_deep(rest_share, grid, at), grid, at)
    out_whole = qkv_whole[:, 3 * head_cols :]
    qkv_whole = qkv_whole[:, : 3 * head_cols]
    up_whole = rest_whole[:, :hidden_cols]

    mod_cols = jnp.dot(condition, w_mod, preferred_element_type=f32) + b_mod.astype(f32)
    own_cols = half_of(mod_cols, side)
    other_cols = swapped(half_of(mod_cols, 1 - side))
    modulation = in_order(
        own_cols.reshape(frames_here, 3, width).transpose(1, 0, 2),
        other_cols.reshape(frames_here, 3, width).transpose(1, 0, 2),
        side,
    )[:, :, None]
    shift_attn, scale_attn, gate_attn, shift_mlp, scale_mlp, gate_mlp = [
        modulation[k] for k in range(6)
    ]

    framed = tokens[0].astype(f32).reshape(frames_here, FRAME, width)
    upstream = cotangent[0].astype(f32).reshape(frames_here, FRAME, width)
    first_own = modulated(framed, shift_attn, scale_attn).astype(bf16).reshape(local_len, width)
    first_full = in_order(first_own, swapped(first_own), side)
    grad_mlp = (gate_mlp * upstream).astype(bf16).reshape(local_len, width)
    grad_mlp_full = jnp.concatenate([grad_mlp, swapped(grad_mlp)], axis=0)

    clip = frame_clip[0]
    order = jnp.arange(clip.shape[0])
    visible = (clip[:, None] == clip[None, :]) & (order[None, :] <= order[:, None])
    seen = frame_lanes(jnp.where(visible, 0.0, hidden_score))
    frames = frame_lanes(jnp.eye(clip.shape[0]))

    qkv = jnp.dot(first_full, qkv_whole, preferred_element_type=f32).astype(bf16)
    part = pairs // 2
    into = attend(qkv, seen, frames, 0, part)
    attended, logs = attend(qkv, seen, frames, part, pairs - part, into)
    branch_other = swapped(nt(half_of(attended, 1 - side), out_whole).astype(bf16))
    branch = nt(half_of(attended, side), out_whole) + branch_other.astype(f32)
    branch = branch.reshape(framed.shape)
    middle = framed + gate_attn * branch
    second_own = modulated(middle, shift_mlp, scale_mlp).astype(bf16).reshape(local_len, width)
    second_full = jnp.concatenate([second_own, swapped(second_own)], axis=0)
    hidden_pre = jnp.dot(second_full, up_whole, preferred_element_type=f32)
    hidden, slope = lax.optimization_barrier(gelu_and_slope(hidden_pre))

    def tn(a, b):
        return lax.dot_general(a, b, (((0,), (0,)), ((), ())), preferred_element_type=f32)

    grad_down = tn(grad_mlp_full, hidden).astype(bf16)
    grad_mlp_full, grad_down = lax.optimization_barrier((grad_mlp_full, grad_down))
    down_sum = lax.psum_scatter(grad_down, "rows", scatter_dimension=0, tiled=True)
    down_sum = down_sum.astype(f32)
    grad_hidden = jnp.dot(grad_mlp_full, down_whole, preferred_element_type=f32)
    grad_pre = (grad_hidden * slope.astype(f32)).astype(bf16)
    second_other = nt(grad_pre[local_len:], up_whole).astype(bf16)
    up_cuts = scatter_cut(tn(second_full, grad_pre).astype(bf16), grid, at)
    second_other, up_cuts = lax.optimization_barrier((second_other, up_cuts))
    up_sum = scatter_rows(up_cuts, grid, at)
    second_other = swapped(second_other)
    grad_second = nt(grad_pre[:local_len], up_whole) + second_other.astype(f32)
    second_back = jax.vjp(modulated, middle, shift_mlp, scale_mlp)[1]
    grad_middle, grad_shift_mlp, grad_scale_mlp = second_back(grad_second.reshape(framed.shape))
    grad_middle = grad_middle + upstream
    grad_gate_attn = jnp.sum(grad_middle * branch, axis=1)
    grad_branch = (gate_attn * grad_middle).astype(bf16).reshape(local_len, width)
    branch_full = in_order(grad_branch, swapped(grad_branch), side)
    grad_out = tn(branch_full, attended).astype(bf16)
    grad_attended = jnp.dot(branch_full, out_whole, preferred_element_type=f32).astype(bf16)
    grad_qkv = attend_back(qkv, seen, frames, logs, grad_attended, 0, part)
    grad_qkv = attend_back(qkv, seen, frames, logs, grad_attended, part, pairs - part, grad_qkv)
    grad_tail = jnp.concatenate([tn(first_full, grad_qkv).astype(bf16), grad_out], axis=1)
    tail_sum = scatter_rows(scatter_cut(grad_tail, grid, at), grid, at)
    qkv_sum, out_sum = tail_sum[:, : 3 * head_cols], tail_sum[:, 3 * head_cols :]
    first_other = swapped(nt(half_of(grad_qkv, 1 - side), qkv_whole).astype(bf16))
    grad_first = nt(half_of(grad_qkv, side), qkv_whole) + first_other.astype(f32)
    hidden_late, grad_qkv = lax.optimization_barrier((hidden, grad_qkv))
    mlp_other = swapped(nt(hidden_late[local_len:], down_whole).astype(bf16))
    mlp_out = nt(hidden_late[:local_len], down_whole) + mlp_other.astype(f32)
    mlp_out = mlp_out.reshape(framed.shape)
    output = (middle + gate_mlp * mlp_out).astype(bf16).reshape(tokens.shape)
    grad_gate_mlp = jnp.sum(upstream * mlp_out, axis=1)

    first_back = jax.vjp(modulated, framed, shift_attn, scale_attn)[1]
    grad_framed, grad_shift_attn, grad_scale_attn = first_back(grad_first.reshape(framed.shape))
    grad_tokens = (grad_framed + grad_middle).astype(bf16).reshape(tokens.shape)

    low = jnp.concatenate([grad_shift_attn, grad_scale_attn, grad_gate_attn[:, None]], axis=-1)
    high = jnp.concatenate([grad_shift_mlp, grad_scale_mlp, grad_gate_mlp[:, None]], axis=-1)
    low, high = low.reshape(frames_here, -1), high.reshape(frames_here, -1)
    keep = jnp.where(side == 0, low, high).astype(bf16)
    give = jnp.where(side == 0, high, low).astype(bf16)
    rest_late, give = lax.optimization_barrier((rest_whole, give))
    condition_all = rest_late[:, hidden_cols:].reshape(-1, width)
    give = swapped(give)
    mine = in_order(keep, give, side)
    grad_mods = gather_rest(gather_deep(mine, grid, at), grid, at)
    mod_sum = tn(condition_all, grad_mods)
    bias_sum = jnp.sum(grad_mods.astype(f32), axis=0)

    qkv_sum = qkv_sum.reshape(share, pairs, 3, PAIR).transpose(0, 2, 1, 3).reshape(w_qkv.shape)
    return (output, grad_tokens, qkv_sum, out_sum.T, up_sum, down_sum.T, mod_sum, bias_sum)


def solution(mesh):
    in_specs = (
        P("rows", "seq", None),
        P("rows", "seq"),
        P("rows", None),
        P("rows", None, "seq"),
        P("seq", "rows"),
        P("rows", "seq"),
        P("seq", "rows"),
        P(None, "seq"),
        P("seq"),
        P("rows", "seq", None),
    )
    out_specs = (
        P("rows", "seq", None),
        P("rows", "seq", None),
        P("rows", None, "seq"),
        P("seq", "rows"),
        P("rows", "seq"),
        P("seq", "rows"),
        P(None, "seq"),
        P("seq"),
    )
    return jax.shard_map(block, mesh=mesh, in_specs=in_specs, out_specs=out_specs, check_vma=False)
```
